512 devices in a mesh: tm: 16 (over x, z_hi), lib: 32 (over y, z_lo, core).
Axes of the slice: x: 4, y: 4, z: 16 (z_hi: 4, z_lo: 4; z = z_hi * 4 + z_lo), core: 2. Of those that a mesh axis runs over, the one named last changes fastest.
Arguments:
- record: bfloat16 [24, 8192], P(None, 'tm'), may hold values from -6 to 6
- templates: bfloat16 [32, 16, 4, 24, 64, 256], P('lib', 'tm'), may hold values from -6 to 6
- owner: int32 [32, 2], P('lib'), may hold values from 0 to 15
- slot: int32 [32, 2], P('lib'), may hold values from 0 to 3
- mask: int32 [24], replicated, may hold values 0 or 1
Outputs:
- stacks: bfloat16 [32, 2, 64, 8192], P('lib', None, None, 'tm')
- best: float32 [8192], P('tm')
The draws below stay inside these ranges and needn't reach their ends.
Inputs may be any that keep to these rules, and one draw needn't show every extreme that they name: owner names a tm index. slot names a held block.
All inputs are finite; a program needn't handle non-finite values.
Results may differ from the reference program's by a relative error of at most 0.005.
Values may be sent and summed in bfloat16 or wider, within the bound.
A program may use at most 64 MiB of HBM per device.

```python
import jax
import jax.numpy as jnp
from jax import lax

C = 24
L = 256
BLOCK = 64
SLOTS = 4
ROUNDS = 2
TIME = 8192
N_TM = 16
N_LIB = 32


def place_ends(values, rng, smallest, high):
    spot = [jax.random.randint(jax.random.fold_in(rng, axis), (), 0, length) for axis, length in enumerate(values.shape)]
    main_axis = values.shape.index(max(values.shape))
    neighbour = spot[:main_axis] + [(spot[main_axis] + 1) % values.shape[main_axis]] + spot[main_axis + 1:]
    return values.at[tuple(spot)].set(smallest).at[tuple(neighbour)].set(high)


def block_levels(stream_key, shape, split, least, largest):
    def one(axis_at, parts):
        heights = jax.random.uniform(jax.random.fold_in(jax.random.fold_in(stream_key, 6), axis_at), (parts,), jnp.float32, least / len(split), largest / len(split))
        return jnp.repeat(jnp.exp(heights), shape[axis_at] // parts).reshape((-1,) + (1,) * (len(shape) - axis_at - 1))

    level = one(*split[0])
    for cut in split[1:]:
        level = level * one(*cut)
    return level


def scatter_about(key, shape, scale, reach, shards=(), kind=jnp.bfloat16):
    entries = jax.random.normal(key, shape, jnp.float32) * scale
    if len(shards) > 0:
        entries = block_levels(key, shape, shards, -0.22, 0.18) * entries
    return jnp.clip(entries, min=-reach, max=reach).astype(kind)


def setup_inputs(seed: int = 0) -> dict:
    splits = jax.random.split(jax.random.key(seed), 6)
    return {
        "record": scatter_about(splits[0], (C, TIME), 1.0, 6.0, ((1, 16),)),
        "templates": scatter_about(splits[1], (N_LIB, N_TM, SLOTS, C, BLOCK, L), 1.0, 6.0, ((0, 32), (1, 16))),
        "owner": place_ends(jax.random.randint(splits[2], (N_LIB, ROUNDS), 0, N_TM), jax.random.fold_in(splits[2], 1), 0, N_TM - 1).astype(jnp.int32),
        "slot": place_ends(jax.random.randint(splits[3], (N_LIB, ROUNDS), 0, SLOTS), jax.random.fold_in(splits[3], 1), 0, SLOTS - 1).astype(jnp.int32),
        "mask": place_ends((jax.random.randint(splits[4], (C,), 0, 4) < 3).astype(jnp.int32), jax.random.fold_in(splits[4], 1), 0, 1),
    }


def grouped_corr(signal, kernel, groups, precision):
    return lax.conv_general_dilated(signal[None], kernel, (1,), 'VALID', dimension_numbers=('NCH', 'OIH', 'NCH'), feature_group_count=groups, precision=precision, preferred_element_type=jnp.float32)[0]

def reference(record, templates, owner, slot, mask):
    padded = jnp.concatenate([record, jnp.zeros((C, L), record.dtype)], axis=1)
    squares = padded.astype(jnp.float32) ** 2
    ones_kernel = jnp.ones((C, 1, L), jnp.float32)
    energy = grouped_corr(squares, ones_kernel, C, lax.Precision.HIGHEST)[:, :TIME]
    weight = mask.astype(jnp.float32)[:, None] / jnp.sqrt(jnp.maximum(energy, jnp.float32(L / 4)))
    count = jnp.maximum(jnp.sum(mask.astype(jnp.float32)), 1.0)
    gain = jnp.sqrt(jnp.float32(L)) / jnp.sqrt(count)

    def one_block(index):
        row = index // ROUNDS
        turn = index % ROUNDS
        holder = owner[row, turn]
        place = slot[row, turn]
        chosen = templates[row][holder][place]
        wide = chosen.astype(jnp.float32)
        norms = jnp.sqrt(lax.optimization_barrier(jnp.sum(wide * wide, axis=-1, keepdims=True)) + 1e-06)
        unit = (wide / norms).astype(jnp.bfloat16)
        kernel = unit.reshape(C * BLOCK, 1, L)
        corr = grouped_corr(padded, kernel, C, None)[:, :TIME].reshape(C, BLOCK, TIME)
        stack_f = lax.optimization_barrier(jnp.sum(corr * weight[:, None, :], axis=0)) * gain
        return (stack_f.astype(jnp.bfloat16), lax.optimization_barrier(jnp.max(stack_f, axis=0)))
    stacked, peaks = lax.map(one_block, jnp.arange(N_LIB * ROUNDS, dtype=jnp.int32))
    stacks = stacked.reshape(N_LIB, ROUNDS, BLOCK, TIME)
    best = lax.optimization_barrier(jnp.max(peaks, axis=0))
    return (stacks, best)
```

```python
import functools

import jax
import jax.numpy as jnp
from jax import lax
from jax.experimental import pallas as pl
from jax.experimental.pallas import tpu as pltpu
from jax.sharding import PartitionSpec as P

MESH = pl.DeviceIdType.MESH
LANES = 128
SHIFTS = 32
PER = 8
PHASES = LANES // SHIFTS
CHUNK = 4


def kernel(
    n_tm, n_lib, rec, tmpl, owner, slot, mask, out, best,
    blk, own, rsx, cand, rsz, recg, g32, s32, left, u32, wt32, nt, wide_t, acc, sbuf, bl_s, bl_r, lb_r,
    t_sem, bz_s, bz_r, bx_s, bx_r, x_s, x_r, z_s, z_r, o_s, o_r, m_s, m_r, l_s, l_r,
):
    slots, channels, block, taps = tmpl.shape
    samples = rec.shape[1]
    me = lax.axis_index("tm")
    lib = lax.axis_index("lib")
    side = 4
    x, z = me // side, lax.rem(me, side)
    chunks = channels // CHUNK
    per_dev = samples // LANES
    rows = n_tm * per_dev

    def at_x(k):
        return {"tm": lax.rem(x + k, side) * side + z}

    def at_z(k):
        return {"tm": x * side + lax.rem(z + k, side)}

    def at_tm(k):
        return {"tm": lax.rem(me + k, n_tm)}

    def at_lib(k):
        return {"lib": lax.rem(lib + k, n_lib)}

    def send(src, dst, s, r, to):
        return pltpu.make_async_remote_copy(
            src_ref=src, dst_ref=dst, send_sem=s, recv_sem=r, device_id=to, device_id_type=MESH
        )

    load = pltpu.make_async_copy(tmpl, blk, t_sem)
    load.start()
    barrier = pltpu.get_barrier_semaphore()
    for k in range(1, n_tm):
        pl.semaphore_signal(barrier, inc=1, device_id=at_tm(k), device_id_type=MESH)
    for k in range(1, n_lib):
        pl.semaphore_signal(barrier, inc=1, device_id=at_lib(k), device_id_type=MESH)

    for ii in range(per_dev):
        recg[me * per_dev + ii] = rec[:, LANES * ii : LANES * (ii + 1)]
    u32[...] = jnp.zeros_like(u32)
    acc[...] = jnp.zeros_like(acc)
    owner_x = [owner[r] // side for r in range(2)]
    owner_z = [lax.rem(owner[r], side) for r in range(2)]
    load.wait()

    def pick(q, _):
        for r in range(2):
            for cc in range(CHUNK):
                for j in range(side):
                    for h in range(2):
                        own[q, j, 2 * r + h, PER * cc : PER * (cc + 1), :] = blk[
                            slot[r], q * CHUNK + cc, (2 * j + h) * PER : (2 * j + h + 1) * PER, :
                        ]
        return 0

    lax.fori_loop(0, chunks, pick, 0)
    pl.semaphore_wait(barrier, n_tm - 1 + n_lib - 1)

    def rec_z(k):
        part = pl.ds(me * per_dev, per_dev)
        return send(recg.at[part], recg.at[part], bz_s.at[k - 1], bz_r.at[k - 1], at_z(k))

    def rec_x(k):
        part = pl.ds(x * side * per_dev, side * per_dev)
        return send(recg.at[part], recg.at[part], bx_s.at[k - 1], bx_r.at[k - 1], at_x(k))

    def tmpl_x(q, k):
        return send(
            own.at[q, lax.rem(x + k, side)], rsx.at[q, k - 1], x_s.at[q, k - 1], x_r.at[q, k - 1], at_x(k)
        )

    def tmpl_z(q, k):
        return send(
            cand.at[q, lax.rem(z + k, side)], rsz.at[q, k - 1], z_s.at[q, k - 1], z_r.at[q, k - 1], at_z(k)
        )

    order = (2, 1, 3)
    early = chunks // 2
    for k in order:
        rec_z(k).start()
    for q in range(early):
        for k in order:
            tmpl_x(q, k).start()
    for k in order:
        rec_z(k).wait_recv()
    for k in order:
        rec_x(k).start()
    for q in range(early, chunks):
        for k in order:
            tmpl_x(q, k).start()

    def pass_on(q):
        for k in order:
            tmpl_x(q, k).wait_recv()
        for i in range(side):
            v = own[q, x, i]
            for k in range(1, side):
                v = jnp.where(owner_x[i // 2] == lax.rem(x + side - k, side), rsx[q, k - 1, i], v)
            cand[q, i] = v
        for k in order:
            tmpl_z(q, k).start()

    lane = lax.broadcasted_iota(jnp.int32, (1, LANES), 1)

    def spread_out(i, _):
        v = recg[i].astype(jnp.float32)
        g32[pl.ds(i * channels, channels), :] = v
        s32[i] = v * v
        return 0

    step = 11
    full = (rows + 2) // step

    def doubled(by, b, _):
        v = s32[pl.ds(b * step, step + 1)]
        r = pltpu.roll(v, LANES - by, axis=2)
        s32[pl.ds(b * step, step)] = v[:step] + jnp.where(lane[None] < LANES - by, r[:step], r[1:])
        return 0

    def weigh(i, _):
        e = s32[i] + s32[i + 1]
        g = 1.0 / jnp.sqrt(jnp.maximum(e, jnp.float32(taps / 4)))
        wt32[pl.ds(i * channels, channels), :] = g
        return 0

    def windows(c, _):
        raw = [g32[pl.ds(c + channels * k, rows, stride=channels), :] for k in range(3)]
        for e in range(PHASES):
            cut = LANES - SHIFTS * e
            v = raw if e == 0 else [pltpu.roll(a, cut, axis=1) for a in raw]
            for p in range(2):
                w = v[p] if e == 0 else jnp.where(lane < cut, v[p], v[p + 1])
                left[c, rows * e : rows * (e + 1), LANES * p : LANES * (p + 1)] = w.astype(jnp.bfloat16)
            left[c, rows * e : rows * (e + 1), 2 * LANES : 3 * LANES] = v[2].astype(jnp.bfloat16)
        return 0

    mine = z // 2
    own_z = jnp.where(mine == 0, owner_z[0], owner_z[1])

    def correlate(q):
        for k in order:
            tmpl_z(q, k).wait_recv()
        v = cand[q, z]
        for k in range(1, side):
            v = jnp.where(own_z == lax.rem(z + side - k, side), rsz[q, k - 1], v)
        wide = v.astype(jnp.float32)
        inv = 1.0 / jnp.sqrt(jnp.sum(wide * wide, axis=1, keepdims=True) + 1e-06)
        u32[:, :taps] = (wide * inv).astype(jnp.bfloat16).astype(jnp.float32)

        def channel(cc, _):
            c = q * CHUNK + cc
            u = u32[pl.ds(pl.multiple_of(cc * PER, PER), PER), :]
            for s in range(SHIFTS):
                w = u if s == 0 else pltpu.roll(u, s, axis=1)
                for p in range(3):
                    wide_t[p, pl.ds(s, PER, stride=SHIFTS), :] = w[:, LANES * p : LANES * (p + 1)]
            right = jnp.concatenate([wide_t[p].astype(jnp.bfloat16) for p in range(3)], axis=1)
            corr = lax.dot_general(
                left[c], right, (((1,), (1,)), ((), ())),
                preferred_element_type=jnp.float32,
            )
            g = wt32[pl.ds(c, rows, stride=channels), :]
            g = jnp.where(mask[c] != 0, g, 0.0)
            turned = [g] + [pltpu.roll(g, SHIFTS * d, axis=1) for d in range(1, PHASES)]
            for e in range(PHASES):
                tile = turned[(PHASES - 1 - e) % PHASES]
                for grp in range(PHASES - 1):
                    tile = jnp.where(lane // SHIFTS == grp, turned[(grp - e) % PHASES], tile)
                both = jnp.concatenate([tile, tile], axis=1)
                part = slice(rows * e, rows * (e + 1))
                acc[part, :] += corr[part, :] * both
            return 0

        lax.fori_loop(0, CHUNK, channel, 0)

    for q in range(early):
        pass_on(q)
    for k in order:
        rec_x(k).wait_recv()
    lax.fori_loop(0, rows, spread_out, 0)
    g32[pl.ds(rows * channels, 8 * channels), :] = jnp.zeros((8 * channels, LANES), jnp.float32)
    s32[pl.ds(rows, 8)] = jnp.zeros((8, channels, LANES), jnp.float32)
    by = 1
    while by < LANES:
        lax.fori_loop(0, full, functools.partial(doubled, by), 0)
        by *= 2
    lax.fori_loop(0, rows, weigh, 0)
    third = channels // (chunks - early)
    for q in range(early, chunks):
        pass_on(q)
        a = (q - early) * third
        lax.fori_loop(a, a + third, windows, 0)
    for q in range(chunks):
        correlate(q)

    count = mask[0]
    for c in range(1, channels):
        count = count + mask[c]
    count_f = jnp.maximum(jnp.full((8, LANES), count, jnp.int32).astype(jnp.float32), 1.0)
    gain = (jnp.sqrt(jnp.float32(taps)) / jnp.sqrt(count_f))[:1]
    top = None
    for m in range(PER):
        h, mm = m // PHASES, m % PHASES
        v = None
        for e in range(PHASES):
            a = acc[rows * e : rows * (e + 1), LANES * h : LANES * (h + 1)]
            by = (SHIFTS * (e - mm)) % LANES
            a = a if by == 0 else pltpu.roll(a, by, axis=1)
            v = a if e == 0 else jnp.where(lane // SHIFTS == e, a, v)
        v = v * gain
        nt[pl.ds(m, rows, stride=PER), :] = v
        top = v if m == 0 else jnp.maximum(top, v)
    for t in range(n_tm):
        bl_s[t] = top[per_dev * t : per_dev * (t + 1), :]
    for t in range(n_tm):
        for ii in range(per_dev):
            a = (per_dev * t + ii) * PER
            sbuf[t, :, LANES * ii : LANES * (ii + 1)] = nt[a : a + PER, :].astype(jnp.bfloat16)

    def peak_tm(k):
        return send(bl_s.at[lax.rem(me + k, n_tm)], bl_r.at[k - 1], m_s.at[k - 1], m_r.at[k - 1], at_tm(k))

    place = out.at[mine, pl.ds(pl.multiple_of((2 * x + lax.rem(z, 2)) * PER, PER), PER), :]

    def stack_tm(k):
        return send(sbuf.at[lax.rem(me + k, n_tm)], place, o_s.at[k - 1], o_r.at[k - 1], at_tm(k))

    for k in range(1, n_tm):
        peak_tm(k).start()
    for k in range(1, n_tm):
        stack_tm(k).start()
    out[mine, pl.ds(pl.multiple_of((2 * x + lax.rem(z, 2)) * PER, PER), PER), :] = sbuf[me]
    peak = bl_s[me]
    for k in range(1, n_tm):
        peak_tm(k).wait_recv()
        peak = jnp.maximum(peak, bl_r[k - 1])
    lb_r[0] = peak

    def peak_lib(k):
        return send(lb_r.at[0], lb_r.at[k], l_s.at[k - 1], l_r.at[k - 1], at_lib(k))

    for k in range(1, n_lib):
        peak_lib(k).start()
    for k in range(1, n_lib):
        peak_lib(k).wait_recv()
        peak = jnp.maximum(peak, lb_r[k])
    best[...] = peak
    for k in range(1, n_tm):
        stack_tm(k).wait_recv()
    for k in order:
        rec_z(k).wait_send()
        rec_x(k).wait_send()
        for q in range(chunks):
            tmpl_x(q, k).wait_send()
            tmpl_z(q, k).wait_send()
    for k in range(1, n_tm):
        peak_tm(k).wait_send()
        stack_tm(k).wait_send()
    for k in range(1, n_lib):
        peak_lib(k).wait_send()


def on_device(record, templates, owner, slot, mask):
    channels, samples = record.shape
    block, taps = templates.shape[-2:]
    rounds = owner.shape[1]
    n_tm, n_lib = lax.axis_size("tm"), lax.axis_size("lib")
    chunks = channels // CHUNK
    per_dev = samples // LANES
    rows = n_tm * per_dev
    vm, bf, f32 = pltpu.VMEM, jnp.bfloat16, jnp.float32
    dma = pltpu.SemaphoreType.DMA
    vmem = pl.BlockSpec(memory_space=pltpu.VMEM)
    smem = pl.BlockSpec(memory_space=pltpu.SMEM)
    piece = (CHUNK * PER, taps)

    stacks, best = pl.pallas_call(
        functools.partial(kernel, n_tm, n_lib),
        out_shape=(
            jax.ShapeDtypeStruct((rounds, block, samples), bf),
            jax.ShapeDtypeStruct((per_dev, LANES), f32),
        ),
        in_specs=[vmem, pl.BlockSpec(memory_space=pl.ANY), smem, smem, smem],
        out_specs=(vmem, vmem),
        scratch_shapes=[
            vm(templates.shape[2:], bf),
            vm((chunks, 4, 4, *piece), bf),
            vm((chunks, 3, 4, *piece), bf),
            vm((chunks, 4, *piece), bf),
            vm((chunks, 3, *piece), bf),
            vm((rows, channels, LANES), bf),
            vm(((rows + 8) * channels, LANES), f32),
            vm((rows + 8, channels, LANES), f32),
            vm((channels, PHASES * rows, 3 * LANES), bf),
            vm((CHUNK * PER, 3 * LANES), f32),
            vm((rows * channels, LANES), f32),
            vm((rows * PER, LANES), f32),
            vm((3, PER * SHIFTS, LANES), f32),
            vm((PHASES * rows, PER * SHIFTS), f32),
            vm((n_tm, PER, samples), bf),
            vm((n_tm, per_dev, LANES), f32),
            vm((n_tm - 1, per_dev, LANES), f32),
            vm((n_lib, per_dev, LANES), f32),
            dma,
            dma((3,)), dma((3,)), dma((3,)), dma((3,)),
            dma((chunks, 3)), dma((chunks, 3)), dma((chunks, 3)), dma((chunks, 3)),
            dma((n_tm - 1,)), dma((n_tm - 1,)), dma((n_tm - 1,)), dma((n_tm - 1,)),
            dma((n_lib - 1,)), dma((n_lib - 1,)),
        ],
        compiler_params=pltpu.CompilerParams(
            collective_id=0, has_side_effects=True, vmem_limit_bytes=48 << 20
        ),
        name="match",
    )(record, templates[0, 0], owner[0], slot[0], mask)
    return stacks[None], best.reshape(samples)


def solution(mesh):
    placed = (
        P(None, "tm"),
        P("lib", "tm", None, None, None, None),
        P("lib", None),
        P("lib", None),
        P(),
    )
    return jax.shard_map(
        on_device,
        mesh=mesh,
        in_specs=placed,
        out_specs=(P("lib", None, None, "tm"), P("tm")),
        check_vma=False,
    )
```

```python
import functools

import jax
import jax.numpy as jnp
from jax import lax
from jax.experimental import pallas as pl
from jax.experimental.pallas import tpu as pltpu
from jax.sharding import PartitionSpec as P

MESH = pl.DeviceIdType.MESH
LANES = 128
HALF = LANES // 2
SHIFTS = 32
PER = 8
SIDE = 4
CHUNK = 2


def kernel(
    n_tm, n_lib, rec_h, tmpl, owner_h, slot_h, mask_h, out, best,
    rec, owner, slot, mask, blk, own, rsx, cand, rsz, recg, g32, right, lhs, wt32, tile, nt, acc,
    sbuf, bl_s, bl_r, near_b, far_b,
    in_sem, bz_s, bz_r, bx_s, bx_r, x_s, x_r, z_s, z_r, o_s, o_r, m_s, m_r, n_s, n_r, f_s, f_r,
):
    slots, channels, block, taps = tmpl.shape
    samples = rec.shape[1]
    me = lax.axis_index("tm")
    lib = lax.axis_index("lib")
    x, z = me // SIDE, lax.rem(me, SIDE)
    near = n_lib // SIDE
    far_at, near_at = lib // near, lax.rem(lib, near)
    chunks = channels // CHUNK
    per_dev = samples // LANES
    rows = n_tm * per_dev
    f32, bf = jnp.float32, jnp.bfloat16

    def at_x(k):
        return {"tm": lax.rem(x + k, SIDE) * SIDE + z}

    def at_z(k):
        return {"tm": x * SIDE + lax.rem(z + k, SIDE)}

    def at_tm(k):
        return {"tm": lax.rem(me + k, n_tm)}

    def at_near(k):
        return {"lib": far_at * near + lax.rem(near_at + k, near)}

    def at_far(k):
        return {"lib": lax.rem(far_at + k, SIDE) * near + near_at}

    def send(src, dst, s, r, to):
        return pltpu.make_async_remote_copy(
            src_ref=src, dst_ref=dst, send_sem=s, recv_sem=r, device_id=to, device_id_type=MESH
        )

    loads = [
        pltpu.make_async_copy(a, b, in_sem.at[n])
        for n, (a, b) in enumerate(
            ((slot_h, slot), (tmpl, blk), (rec_h, rec), (owner_h, owner), (mask_h, mask))
        )
    ]
    barrier = pltpu.get_barrier_semaphore()
    peers = [at_z(k) for k in range(1, SIDE)] + [at_x(k) for k in range(1, SIDE)]
    peers += [at_near(k) for k in range(1, near)] + [at_far(k) for k in range(1, SIDE)]
    for to in peers:
        pl.semaphore_signal(barrier, inc=1, device_id=to, device_id_type=MESH)
    for copy in loads:
        copy.start()

    lane = lax.broadcasted_iota(jnp.int32, (1, LANES), 1)
    acc[...] = jnp.zeros_like(acc)
    used = taps + SHIFTS
    right[:, used:, :] = jnp.zeros((channels, right.shape[1] - used, 2 * LANES), bf)
    g32[pl.ds(rows * channels, (LANES - rows) * channels), :] = jnp.zeros(
        ((LANES - rows) * channels, LANES), f32
    )
    for n in (0, 2, 3, 4):
        loads[n].wait()
    for ii in range(per_dev):
        recg[me * per_dev + ii] = rec[:, LANES * ii : LANES * (ii + 1)]
    owner_x = [owner[0, r] // SIDE for r in range(2)]
    owner_z = [lax.rem(owner[0, r], SIDE) for r in range(2)]
    loads[1].wait()

    def pick(q, _):
        for r in range(2):
            for cc in range(CHUNK):
                for j in range(SIDE):
                    for h in range(2):
                        own[q, j, 2 * r + h, PER * cc : PER * (cc + 1), :] = blk[
                            slot[0, r], q * CHUNK + cc, (2 * j + h) * PER : (2 * j + h + 1) * PER, :
                        ]
        return 0

    lax.fori_loop(0, chunks, pick, 0)
    pl.semaphore_wait(barrier, len(peers))

    def rec_z(k):
        part = pl.ds(me * per_dev, per_dev)
        return send(recg.at[part], recg.at[part], bz_s.at[k - 1], bz_r.at[k - 1], at_z(k))

    def rec_x(k):
        part = pl.ds(x * SIDE * per_dev, SIDE * per_dev)
        return send(recg.at[part], recg.at[part], bx_s.at[k - 1], bx_r.at[k - 1], at_x(k))

    def tmpl_x(q, k):
        return send(
            own.at[q, lax.rem(x + k, SIDE)], rsx.at[q, k - 1], x_s.at[q, k - 1], x_r.at[q, k - 1], at_x(k)
        )

    def tmpl_z(q, k):
        return send(
            cand.at[q, lax.rem(z + k, SIDE)], rsz.at[q, k - 1], z_s.at[q, k - 1], z_r.at[q, k - 1], at_z(k)
        )

    order = (2, 1, 3)

    def start_x(a, b):
        for q in range(a, b):
            for k in order:
                tmpl_x(q, k).start()

    def pass_on(a, b):
        for q in range(a, b):
            for k in order:
                tmpl_x(q, k).wait_recv()
            for i in range(SIDE):
                v = own[q, x, i]
                for k in range(1, SIDE):
                    v = jnp.where(owner_x[i // 2] == lax.rem(x + SIDE - k, SIDE), rsx[q, k - 1, i], v)
                cand[q, i] = v
            for k in order:
                tmpl_z(q, k).start()

    group = 8

    def spread_out(b, _):
        for n in range(group):
            i = b * group + n
            v = recg[i].astype(f32)
            g32[pl.ds(pl.multiple_of(i * channels, 8), channels), :] = v
        return 0

    def weigh(b, band):
        n = group * channels
        a = pl.multiple_of(b * n, 8)
        top, rest = [], []
        for k in range(3):
            v = g32[pl.ds(a + channels * k, n), :]
            sq = v * v
            top.append(sq.astype(bf))
            rest.append((sq - top[k].astype(f32)).astype(bf))
        e = jnp.dot(jnp.concatenate(top, axis=1), band, preferred_element_type=f32)
        e = e + jnp.dot(jnp.concatenate(rest, axis=1), band, preferred_element_type=f32)
        wt32[pl.ds(a, n), :] = 1.0 / jnp.sqrt(jnp.maximum(e, jnp.float32(taps / 4)))
        return band

    def windows(c, _):
        t0 = g32[pl.ds(c, LANES, stride=channels), :].T
        flat = jnp.concatenate([t0] + [pltpu.roll(t0, LANES - k, axis=1) for k in (1, 2)], axis=0)
        turned = jnp.concatenate([pltpu.roll(t0, HALF - k, axis=1) for k in range(3)], axis=0)
        for p in range(2):
            a = 2 * SHIFTS * p
            w = jnp.where(lane < HALF, flat[a : a + used], turned[a + SHIFTS : a + SHIFTS + used])
            right[c, :used, LANES * p : LANES * (p + 1)] = w.astype(bf)
        g = wt32[pl.ds(c, rows, stride=channels), :]
        g = jnp.where(mask[c] != 0, g, 0.0)
        g = jnp.concatenate([g, jnp.zeros((LANES - rows, LANES), f32)], axis=0).T
        for p in range(2):
            a = 2 * SHIFTS * p
            tile[c, p] = jnp.where(
                lane < HALF, g[a : a + SHIFTS], pltpu.roll(g[a + SHIFTS : a + 2 * SHIFTS], HALF, axis=1)
            )
        return 0

    mine = z // 2
    own_z = jnp.where(mine == 0, owner_z[0], owner_z[1])

    def correlate(q, _):
        for k in order:
            tmpl_z(q, k).wait_recv()
        v = cand[q, z]
        for k in range(1, SIDE):
            v = jnp.where(own_z == lax.rem(z + SIDE - k, SIDE), rsz[q, k - 1], v)
        wide = v.astype(f32)
        inv = 1.0 / jnp.sqrt(jnp.sum(wide * wide, axis=1, keepdims=True) + 1e-06)
        unit = (wide * inv).astype(bf).astype(f32)
        for cc in range(CHUNK):
            c = q * CHUNK + cc
            u0 = unit[PER * cc : PER * (cc + 1), :LANES]
            u1 = unit[PER * cc : PER * (cc + 1), LANES:]
            for s in range(0, SHIFTS, 2):
                cols = [[], [], []]
                for b in (s, s + 1):
                    r0 = u0 if b == 0 else pltpu.roll(u0, b, axis=1)
                    r1 = u1 if b == 0 else pltpu.roll(u1, b, axis=1)
                    cols[0].append(jnp.where(lane < b, 0.0, r0))
                    cols[1].append(jnp.where(lane < b, r0, r1))
                    cols[2].append(jnp.where(lane < b, r1, 0.0))
                for p in range(3):
                    lhs[cc, PER * s : PER * (s + 2), LANES * p : LANES * (p + 1)] = jnp.concatenate(
                        cols[p], axis=0
                    ).astype(bf)
            corr = jnp.dot(lhs[cc], right[c], preferred_element_type=f32)
            for p in range(2):
                for s in range(SHIFTS):
                    part = slice(PER * s, PER * (s + 1))
                    acc[p, part, :] += corr[part, LANES * p : LANES * (p + 1)] * tile[c, p, s : s + 1, :]
        return 0

    def correlate_span(a, b):
        lax.fori_loop(a, b, correlate, 0)

    for k in order:
        rec_z(k).start()
    start_x(0, 7)
    pass_on(0, 2)
    for k in order:
        rec_z(k).wait_recv()
    for k in order:
        rec_x(k).start()
    start_x(7, chunks)
    pass_on(2, 7)
    for k in order:
        rec_x(k).wait_recv()
    lax.fori_loop(0, rows // group, spread_out, 0)
    pass_on(7, 8)
    at_p = lax.broadcasted_iota(jnp.int32, (3 * LANES, LANES), 0)
    at_l = lax.broadcasted_iota(jnp.int32, (3 * LANES, LANES), 1)
    band = jnp.where((at_p >= at_l) & (at_p < at_l + taps), 1.0, 0.0).astype(bf)
    lax.fori_loop(0, rows // group, weigh, band)
    pass_on(8, 10)
    lax.fori_loop(0, channels // 2, windows, 0)
    pass_on(10, chunks)
    lax.fori_loop(channels // 2, channels, windows, 0)
    correlate_span(0, chunks)

    count = mask[0]
    for c in range(1, channels):
        count = count + mask[c]
    count_f = jnp.maximum(jnp.full((8, LANES), count, jnp.int32).astype(f32), 1.0)
    gain = (jnp.sqrt(jnp.float32(taps)) / jnp.sqrt(count_f))[:1]
    top = None
    for m in range(PER):
        a, b = (acc[p, pl.ds(m, SHIFTS, stride=PER), :] for p in range(2))
        v = jnp.concatenate([a, pltpu.roll(a, HALF, axis=1), b, pltpu.roll(b, HALF, axis=1)], axis=0)
        v = v.T[:rows] * gain
        nt[pl.ds(m, rows, stride=PER), :] = v
        top = v if m == 0 else jnp.maximum(top, v)
    for t in range(n_tm):
        bl_s[t] = top[per_dev * t : per_dev * (t + 1), :]

    def peak_tm(k):
        return send(bl_s.at[lax.rem(me + k, n_tm)], bl_r.at[k - 1], m_s.at[k - 1], m_r.at[k - 1], at_tm(k))

    place = out.at[mine, pl.ds(pl.multiple_of((2 * x + lax.rem(z, 2)) * PER, PER), PER), :]

    def stack_tm(k):
        return send(sbuf.at[lax.rem(me + k, n_tm)], place, o_s.at[k - 1], o_r.at[k - 1], at_tm(k))

    for k in range(1, n_tm):
        peak_tm(k).start()
    for t in range(n_tm):
        for ii in range(per_dev):
            a = (per_dev * t + ii) * PER
            sbuf[t, :, LANES * ii : LANES * (ii + 1)] = nt[a : a + PER, :].astype(bf)
    for k in range(1, n_tm):
        stack_tm(k).start()
    out[mine, pl.ds(pl.multiple_of((2 * x + lax.rem(z, 2)) * PER, PER), PER), :] = sbuf[me]
    peak = bl_s[me]
    for k in range(1, n_tm):
        peak_tm(k).wait_recv()
        peak = jnp.maximum(peak, bl_r[k - 1])
    near_b[0] = peak

    def peak_near(k):
        return send(near_b.at[0], near_b.at[k], n_s.at[k - 1], n_r.at[k - 1], at_near(k))

    def peak_far(k):
        return send(far_b.at[0], far_b.at[k], f_s.at[k - 1], f_r.at[k - 1], at_far(k))

    for k in range(1, near):
        peak_near(k).start()
    for k in range(1, near):
        peak_near(k).wait_recv()
        peak = jnp.maximum(peak, near_b[k])
    far_b[0] = peak
    for k in range(1, SIDE):
        peak_far(k).start()
    for k in range(1, SIDE):
        peak_far(k).wait_recv()
        peak = jnp.maximum(peak, far_b[k])
    best[...] = peak
    for k in range(1, n_tm):
        stack_tm(k).wait_recv()
    for k in order:
        rec_z(k).wait_send()
        rec_x(k).wait_send()
        for q in range(chunks):
            tmpl_x(q, k).wait_send()
            tmpl_z(q, k).wait_send()
    for k in range(1, n_tm):
        peak_tm(k).wait_send()
        stack_tm(k).wait_send()
    for k in range(1, near):
        peak_near(k).wait_send()
    for k in range(1, SIDE):
        peak_far(k).wait_send()


def on_device(record, templates, owner, slot, mask):
    channels, samples = record.shape
    block, taps = templates.shape[-2:]
    rounds = owner.shape[1]
    n_tm, n_lib = lax.axis_size("tm"), lax.axis_size("lib")
    chunks = channels // CHUNK
    per_dev = samples // LANES
    rows = n_tm * per_dev
    near = n_lib // SIDE
    vm, bf, f32 = pltpu.VMEM, jnp.bfloat16, jnp.float32
    dma = pltpu.SemaphoreType.DMA
    vmem = pl.BlockSpec(memory_space=pltpu.VMEM)
    hbm = pl.BlockSpec(memory_space=pltpu.MemorySpace.HBM)
    piece = (CHUNK * PER, taps)

    stacks, best = pl.pallas_call(
        functools.partial(kernel, n_tm, n_lib),
        out_shape=(
            jax.ShapeDtypeStruct((rounds, block, samples), bf),
            jax.ShapeDtypeStruct((per_dev, LANES), f32),
        ),
        in_specs=[hbm] * 5,
        out_specs=(vmem, vmem),
        scratch_shapes=[
            vm((channels, samples), bf),
            pltpu.SMEM(owner.shape, jnp.int32),
            pltpu.SMEM(slot.shape, jnp.int32),
            pltpu.SMEM(mask.shape, jnp.int32),
            vm(templates.shape[2:], bf),
            vm((chunks, SIDE, SIDE, *piece), bf),
            vm((chunks, SIDE - 1, SIDE, *piece), bf),
            vm((chunks, SIDE, *piece), bf),
            vm((chunks, SIDE - 1, *piece), bf),
            vm((rows, channels, LANES), bf),
            vm((LANES * channels, LANES), f32),
            vm((channels, 3 * LANES, 2 * LANES), bf),
            vm((CHUNK, SHIFTS * PER, 3 * LANES), bf),
            vm((rows * channels, LANES), f32),
            vm((channels, 2, SHIFTS, LANES), f32),
            vm((rows * PER, LANES), f32),
            vm((2, SHIFTS * PER, LANES), f32),
            vm((n_tm, PER, samples), bf),
            vm((n_tm, per_dev, LANES), f32),
            vm((n_tm - 1, per_dev, LANES), f32),
            vm((near, per_dev, LANES), f32),
            vm((SIDE, per_dev, LANES), f32),
            dma((5,)),
            dma((3,)), dma((3,)), dma((3,)), dma((3,)),
            dma((chunks, 3)), dma((chunks, 3)), dma((chunks, 3)), dma((chunks, 3)),
            dma((n_tm - 1,)), dma((n_tm - 1,)), dma((n_tm - 1,)), dma((n_tm - 1,)),
            dma((near - 1,)), dma((near - 1,)), dma((3,)), dma((3,)),
        ],
        compiler_params=pltpu.CompilerParams(
            collective_id=0, has_side_effects=True, vmem_limit_bytes=48 << 20
        ),
        name="match",
    )(*(pltpu.with_memory_space_constraint(a, pltpu.MemorySpace.HBM) for a in (record, templates[0, 0], owner, slot, mask)))
    return stacks[None], best.reshape(samples)


def solution(mesh):
    placed = (
        P(None, "tm"),
        P("lib", "tm", None, None, None, None),
        P("lib", None),
        P("lib", None),
        P(),
    )
    return jax.shard_map(
        on_device,
        mesh=mesh,
        in_specs=placed,
        out_specs=(P("lib", None, None, "tm"), P("tm")),
        check_vma=False,
    )
```

```python
import functools

import jax
import jax.numpy as jnp
from jax import lax
from jax.experimental import pallas as pl
from jax.experimental.pallas import tpu as pltpu
from jax.sharding import PartitionSpec as P

MESH = pl.DeviceIdType.MESH
LANES = 128
HALF = LANES // 2
SHIFTS = 32
PER = 8
SIDE = 4
CHUNK = 2
DEPTH = 4


def kernel(
    n_tm, n_lib, rec_h, tmpl, owner_h, slot_h, mask_h, out, best,
    rec, owner, slot, mask, blk, own, rsx, cand, rsz, recg, g32, right, lhs, wt32, tile, nt, acc,
    sbuf, pa_s, pa_r, pb_s, pb_r,
    in_sem, bz_s, bz_r, bx_s, bx_r, x_s, x_r, z_s, z_r, o_s, o_r, m_s, m_r, n_s, n_r, bc_s, bc_r,
):
    slots, channels, block, taps = tmpl.shape
    samples = rec.shape[1]
    me = lax.axis_index("tm")
    lib = lax.axis_index("lib")
    x, z = me // SIDE, lax.rem(me, SIDE)
    near = n_lib // SIDE
    far_at, near_at = lib // near, lax.rem(lib, near)
    chunks = channels // CHUNK
    per_dev = samples // LANES
    rows = n_tm * per_dev
    f32, bf = jnp.float32, jnp.bfloat16

    def at_x(k):
        return {"tm": lax.rem(x + k, SIDE) * SIDE + z}

    def at_z(k):
        return {"tm": x * SIDE + lax.rem(z + k, SIDE)}

    def at_tm(k):
        return {"tm": lax.rem(me + k, n_tm)}

    def at_plane(k):
        kx, ky = k // SIDE, k % SIDE
        return {
            "tm": lax.rem(x + kx, SIDE) * SIDE + z,
            "lib": lax.rem(far_at + ky, SIDE) * near + near_at,
        }

    def column(k):
        return lax.rem(z * near + near_at + k, SIDE * near)

    def at_column(k):
        to = column(k)
        return {"tm": x * SIDE + to // near, "lib": far_at * near + lax.rem(to, near)}

    core = lax.rem(near_at, 2)

    def send(src, dst, s, r, to):
        return pltpu.make_async_remote_copy(
            src_ref=src, dst_ref=dst, send_sem=s, recv_sem=r, device_id=to, device_id_type=MESH
        )

    loads = [
        pltpu.make_async_copy(a, b, in_sem.at[n])
        for n, (a, b) in enumerate(
            ((slot_h, slot), (tmpl, blk), (rec_h, rec), (owner_h, owner), (mask_h, mask))
        )
    ]
    for copy in loads:
        copy.start()
    barrier = pltpu.get_barrier_semaphore()
    peers = [at_column(k) for k in range(1, SIDE * near)] + [at_plane(k) for k in range(1, SIDE * SIDE)]
    for to in peers:
        pl.semaphore_signal(barrier, inc=1, device_id=to, device_id_type=MESH)

    lane = lax.broadcasted_iota(jnp.int32, (1, LANES), 1)
    acc[...] = jnp.zeros_like(acc)
    used = taps + SHIFTS
    right[:, used:, :] = jnp.zeros((channels, right.shape[1] - used, 2 * LANES), bf)
    g32[pl.ds(rows * channels, 2 * channels), :] = jnp.zeros((2 * channels, LANES), f32)
    for n in (0, 2, 3, 4):
        loads[n].wait()
    half = per_dev // 2
    for ii in range(half):
        for at_core in range(2):

            @pl.when(core == at_core)
            def _():
                a = LANES * (at_core * half + ii)
                recg[me, at_core, ii] = rec[:, a : a + LANES]

    owner_x = [owner[0, r] // SIDE for r in range(2)]
    owner_z = [lax.rem(owner[0, r], SIDE) for r in range(2)]
    loads[1].wait()

    def pick(q, _):
        for r in range(2):
            for cc in range(CHUNK):
                for j in range(SIDE):
                    for h in range(2):
                        own[q, j, 2 * r + h, PER * cc : PER * (cc + 1), :] = blk[
                            slot[0, r], q * CHUNK + cc, (2 * j + h) * PER : (2 * j + h + 1) * PER, :
                        ]
        return 0

    lax.fori_loop(0, chunks, pick, 0)
    pl.semaphore_wait(barrier, len(peers))

    def rec_z(k):
        part = recg.at[me, core]
        return send(part, part, bz_s.at[k - 1], bz_r.at[k - 1], at_z(k))

    def rec_x(k):
        part = recg.at[pl.ds(x * SIDE, SIDE), core]
        return send(part, part, bx_s.at[k - 1], bx_r.at[k - 1], at_x(k))

    def rec_core():
        part = recg.at[:, core]
        to = {"lib": lib + 1 - 2 * core}
        return send(part, part, bc_s, bc_r, to)

    def tmpl_x(q, k):
        return send(
            own.at[q, lax.rem(x + k, SIDE)], rsx.at[q, k - 1], x_s.at[q, k - 1], x_r.at[q, k - 1], at_x(k)
        )

    def tmpl_z(q, k):
        return send(
            cand.at[q, lax.rem(z + k, SIDE)], rsz.at[q, k - 1], z_s.at[q, k - 1], z_r.at[q, k - 1], at_z(k)
        )

    order = (2, 1, 3)

    def start_x(a, b):
        for q in range(a, b):
            for k in order:
                tmpl_x(q, k).start()

    def pass_on(a, b):
        for q in range(a, b):
            for k in order:
                tmpl_x(q, k).wait_recv()
            for i in range(SIDE):
                v = own[q, x, i]
                for k in range(1, SIDE):
                    v = jnp.where(owner_x[i // 2] == lax.rem(x + SIDE - k, SIDE), rsx[q, k - 1, i], v)
                cand[q, i] = v
            for k in order:
                tmpl_z(q, k).start()

    group = 8

    def spread_out(b, _):
        for n in range(group):
            i = b * group + n
            v = recg[i // per_dev, lax.rem(i, per_dev) // half, lax.rem(i, half)].astype(f32)
            g32[pl.ds(pl.multiple_of(i * channels, 8), channels), :] = v
        return 0

    def weigh(b, band):
        n = group * channels
        a = pl.multiple_of(b * n, 8)
        top, rest = [], []
        for k in range(3):
            v = g32[pl.ds(a + channels * k, n), :]
            sq = v * v
            top.append(sq.astype(bf))
            rest.append((sq - top[k].astype(f32)).astype(bf))
        e = jnp.dot(jnp.concatenate(top, axis=1), band, preferred_element_type=f32)
        e = e + jnp.dot(jnp.concatenate(rest, axis=1), band, preferred_element_type=f32)
        wt32[pl.ds(a, n), :] = 1.0 / jnp.sqrt(jnp.maximum(e, jnp.float32(taps / 4)))
        return band

    def windows(b, _):
        c = 2 * b
        raw = [g32[pl.ds(c + n, rows, stride=channels), :] for n in range(2)]
        t0 = jnp.concatenate(raw, axis=0).T
        at = lax.rem(lane, HALF)
        flat = [t0] + [jnp.where(at < HALF - k, pltpu.roll(t0, LANES - k, axis=1), 0.0) for k in (1, 2)]
        turned = jnp.concatenate([pltpu.roll(t, HALF, axis=1) for t in flat], axis=0)
        flat = jnp.concatenate(flat, axis=0)
        g = [
            jnp.where(mask[c + n] != 0, wt32[pl.ds(c + n, rows, stride=channels), :], 0.0) for n in range(2)
        ]
        g = jnp.concatenate(g, axis=0).T
        g_turned = pltpu.roll(g, HALF, axis=1)
        for n, (f, t, gf, gt) in enumerate(((flat, turned, g, g_turned), (turned, flat, g_turned, g))):
            for p in range(2):
                a = 2 * SHIFTS * p
                w = jnp.where(lane < HALF, f[a : a + used], t[a + SHIFTS : a + SHIFTS + used])
                right[c + n, :used, LANES * p : LANES * (p + 1)] = w.astype(bf)
                tile[c + n, p] = jnp.where(lane < HALF, gf[a : a + SHIFTS], gt[a + SHIFTS : a + 2 * SHIFTS])
        return 0

    mine = z // 2
    own_z = jnp.where(mine == 0, owner_z[0], owner_z[1])

    def build(q, _):
        for k in order:
            tmpl_z(q, k).wait_recv()
        v = cand[q, z]
        for k in range(1, SIDE):
            v = jnp.where(own_z == lax.rem(z + SIDE - k, SIDE), rsz[q, k - 1], v)
        wide = v.astype(f32)
        inv = 1.0 / jnp.sqrt(jnp.sum(wide * wide, axis=1, keepdims=True) + 1e-06)
        unit = (wide * inv).astype(bf).astype(f32)
        for cc in range(CHUNK):
            c = q * CHUNK + cc
            u0 = unit[PER * cc : PER * (cc + 1), :LANES]
            u1 = unit[PER * cc : PER * (cc + 1), LANES:]
            for s in range(0, SHIFTS, 2):
                cols = [[], [], []]
                for b in (s, s + 1):
                    r0 = u0 if b == 0 else pltpu.roll(u0, b, axis=1)
                    r1 = u1 if b == 0 else pltpu.roll(u1, b, axis=1)
                    cols[0].append(jnp.where(lane < b, 0.0, r0))
                    cols[1].append(jnp.where(lane < b, r0, r1))
                    cols[2].append(jnp.where(lane < b, r1, 0.0))
                for p in range(3):
                    lhs[c, PER * s : PER * (s + 2), LANES * p : LANES * (p + 1)] = jnp.concatenate(
                        cols[p], axis=0
                    ).astype(bf)
        return 0

    def multiply(q, _):
        corr = [jnp.dot(lhs[q * CHUNK + n], right[q * CHUNK + n], preferred_element_type=f32) for n in range(CHUNK)]
        for p in range(2):
            for s in range(SHIFTS):
                part, cols = slice(PER * s, PER * (s + 1)), slice(LANES * p, LANES * (p + 1))
                v = acc[p, part, :]
                for n in range(CHUNK):
                    v = v + corr[n][part, cols] * tile[q * CHUNK + n, p, s : s + 1, :]
                acc[p, part, :] = v
        return 0

    def both(q, _):
        build(q, 0)
        multiply(q, 0)
        return 0

    def step(a, b):
        for q in range(a, b):
            pass_on(q, q + 1)
            if q + DEPTH < chunks:
                start_x(q + DEPTH, q + DEPTH + 1)

    at_p = lax.broadcasted_iota(jnp.int32, (3 * LANES, LANES), 0)
    at_l = lax.broadcasted_iota(jnp.int32, (3 * LANES, LANES), 1)
    band = jnp.where((at_p >= at_l) & (at_p < at_l + taps), 1.0, 0.0).astype(bf)
    pairs, blocks = channels // 2, rows // group

    for k in order:
        rec_z(k).start()
    start_x(0, DEPTH)
    step(0, 4)
    for k in order:
        rec_z(k).wait_recv()
    for k in order:
        rec_x(k).start()
    step(4, 6)
    build(0, 0)
    step(6, 7)
    build(1, 0)
    step(7, 8)
    for k in order:
        rec_x(k).wait_recv()
    rec_core().start()
    step(8, 9)
    rec_core().wait_recv()
    lax.fori_loop(0, blocks, spread_out, 0)
    lax.fori_loop(0, blocks // 2, weigh, band)
    step(9, 10)
    lax.fori_loop(blocks // 2, blocks, weigh, band)
    step(10, 11)
    lax.fori_loop(0, pairs // 2, windows, 0)
    step(11, 12)
    lax.fori_loop(pairs // 2, pairs, windows, 0)
    lax.fori_loop(0, 2, multiply, 0)
    lax.fori_loop(2, chunks, both, 0)

    count = mask[0]
    for c in range(1, channels):
        count = count + mask[c]
    count_f = jnp.maximum(jnp.full((8, LANES), count, jnp.int32).astype(f32), 1.0)
    gain = (jnp.sqrt(jnp.float32(taps)) / jnp.sqrt(count_f))[:1]
    def natural(a, b):
        v = jnp.concatenate([a, pltpu.roll(a, HALF, axis=1), b, pltpu.roll(b, HALF, axis=1)], axis=0)
        return v.T[:rows] * gain

    def template(p, m):
        return acc[p, pl.ds(m, SHIFTS, stride=PER), :]

    top = natural(*(functools.reduce(jnp.maximum, [template(p, m) for m in range(PER)]) for p in range(2)))
    for t in range(SIDE):
        pa_s[t] = top[per_dev * SIDE * t : per_dev * SIDE * (t + 1), :]

    def peak_plane(k):
        return send(pa_s.at[lax.rem(x + k // SIDE, SIDE)], pa_r.at[k - 1], m_s.at[k - 1], m_r.at[k - 1], at_plane(k))

    def peak_column(k):
        return send(pb_s.at[column(k) // near], pb_r.at[k - 1], n_s.at[k - 1], n_r.at[k - 1], at_column(k))

    place = out.at[mine, pl.ds(pl.multiple_of((2 * x + lax.rem(z, 2)) * PER, PER), PER), :]

    def stack_tm(k):
        return send(sbuf.at[lax.rem(me + k, n_tm)], place, o_s.at[k - 1], o_r.at[k - 1], at_tm(k))

    for k in range(1, SIDE * SIDE):
        peak_plane(k).start()
    for m in range(PER):
        nt[pl.ds(m, rows, stride=PER), :] = natural(template(0, m), template(1, m))
    for t in range(n_tm):
        for ii in range(per_dev):
            a = (per_dev * t + ii) * PER
            sbuf[t, :, LANES * ii : LANES * (ii + 1)] = nt[a : a + PER, :].astype(bf)
    for k in range(1, n_tm):
        stack_tm(k).start()
    out[mine, pl.ds(pl.multiple_of((2 * x + lax.rem(z, 2)) * PER, PER), PER), :] = sbuf[me]
    peak = pa_s[x]
    for k in range(1, SIDE * SIDE):
        peak_plane(k).wait_recv()
        peak = jnp.maximum(peak, pa_r[k - 1])
    for t in range(SIDE):
        pb_s[t] = peak[per_dev * t : per_dev * (t + 1), :]
    for k in range(1, SIDE * near):
        peak_column(k).start()
    peak = pb_s[z]
    for k in range(1, SIDE * near):
        peak_column(k).wait_recv()
        peak = jnp.maximum(peak, pb_r[k - 1])
    best[...] = peak
    for k in range(1, n_tm):
        stack_tm(k).wait_recv()
    for k in order:
        rec_z(k).wait_send()
        rec_x(k).wait_send()
        for q in range(chunks):
            tmpl_x(q, k).wait_send()
            tmpl_z(q, k).wait_send()
    rec_core().wait_send()
    for k in range(1, n_tm):
        stack_tm(k).wait_send()
    for k in range(1, SIDE * SIDE):
        peak_plane(k).wait_send()
    for k in range(1, SIDE * near):
        peak_column(k).wait_send()


def on_device(record, templates, owner, slot, mask):
    channels, samples = record.shape
    block, taps = templates.shape[-2:]
    rounds = owner.shape[1]
    n_tm, n_lib = lax.axis_size("tm"), lax.axis_size("lib")
    chunks = channels // CHUNK
    per_dev = samples // LANES
    rows = n_tm * per_dev
    near = n_lib // SIDE
    vm, bf, f32 = pltpu.VMEM, jnp.bfloat16, jnp.float32
    dma = pltpu.SemaphoreType.DMA
    vmem = pl.BlockSpec(memory_space=pltpu.VMEM)
    hbm = pl.BlockSpec(memory_space=pltpu.MemorySpace.HBM)
    piece = (CHUNK * PER, taps)

    stacks, best = pl.pallas_call(
        functools.partial(kernel, n_tm, n_lib),
        out_shape=(
            jax.ShapeDtypeStruct((rounds, block, samples), bf),
            jax.ShapeDtypeStruct((per_dev, LANES), f32),
        ),
        in_specs=[hbm] * 5,
        out_specs=(vmem, vmem),
        scratch_shapes=[
            vm((channels, samples), bf),
            pltpu.SMEM(owner.shape, jnp.int32),
            pltpu.SMEM(slot.shape, jnp.int32),
            pltpu.SMEM(mask.shape, jnp.int32),
            vm(templates.shape[2:], bf),
            vm((chunks, SIDE, SIDE, *piece), bf),
            vm((chunks, SIDE - 1, SIDE, *piece), bf),
            vm((chunks, SIDE, *piece), bf),
            vm((chunks, SIDE - 1, *piece), bf),
            vm((n_tm, 2, per_dev // 2, channels, LANES), bf),
            vm(((rows + 2) * channels, LANES), f32),
            vm((channels, 3 * LANES, 2 * LANES), bf),
            vm((channels, SHIFTS * PER, 3 * LANES), bf),
            vm((rows * channels, LANES), f32),
            vm((channels, 2, SHIFTS, LANES), f32),
            vm((rows * PER, LANES), f32),
            vm((2, SHIFTS * PER, LANES), f32),
            vm((n_tm, PER, samples), bf),
            vm((SIDE, SIDE * per_dev, LANES), f32),
            vm((SIDE * SIDE - 1, SIDE * per_dev, LANES), f32),
            vm((SIDE, per_dev, LANES), f32),
            vm((SIDE * near - 1, per_dev, LANES), f32),
            dma((5,)),
            dma((3,)), dma((3,)), dma((3,)), dma((3,)),
            dma((chunks, 3)), dma((chunks, 3)), dma((chunks, 3)), dma((chunks, 3)),
            dma((n_tm - 1,)), dma((n_tm - 1,)), dma((SIDE * SIDE - 1,)), dma((SIDE * SIDE - 1,)),
            dma((SIDE * near - 1,)), dma((SIDE * near - 1,)), dma, dma,
        ],
        compiler_params=pltpu.CompilerParams(
            collective_id=0, has_side_effects=True, vmem_limit_bytes=48 << 20
        ),
        name="match",
    )(*(pltpu.with_memory_space_constraint(a, pltpu.MemorySpace.HBM) for a in (record, templates[0, 0], owner, slot, mask)))
    return stacks[None], best.reshape(samples)


def solution(mesh):
    placed = (
        P(None, "tm"),
        P("lib", "tm", None, None, None, None),
        P("lib", None),
        P("lib", None),
        P(),
    )
    return jax.shard_map(
        on_device,
        mesh=mesh,
        in_specs=placed,
        out_specs=(P("lib", None, None, "tm"), P("tm")),
        check_vma=False,
    )
```

```python
import functools

import jax
import jax.numpy as jnp
from jax import lax
from jax.experimental import pallas as pl
from jax.experimental.pallas import tpu as pltpu
from jax.sharding import PartitionSpec as P

MESH = pl.DeviceIdType.MESH
LANES = 128
HALF = LANES // 2
SHIFTS = 32
PER = 8
SIDE = 4
CHUNK = 2
DEPTH = 4


def kernel(
    n_tm, n_lib, rec_h, tmpl, owner_h, slot_h, mask_h, out, best,
    rec, owner, slot, mask, blk, own, rsx, cand, rsz, recg, g32, right, lhs, wt32, tile, nt, acc,
    sbuf, pa_s, pa_r, pb_s, pb_r,
    in_sem, bz_s, bz_r, bx_s, bx_r, x_s, x_r, z_s, z_r, o_s, o_r, m_s, m_r, n_s, n_r, bc_s, bc_r, vouch,
):
    slots, channels, block, taps = tmpl.shape
    samples = rec.shape[1]
    me = lax.axis_index("tm")
    lib = lax.axis_index("lib")
    x, z = me // SIDE, lax.rem(me, SIDE)
    near = n_lib // SIDE
    far_at, near_at = lib // near, lax.rem(lib, near)
    chunks = channels // CHUNK
    per_dev = samples // LANES
    rows = n_tm * per_dev
    f32, bf = jnp.float32, jnp.bfloat16

    def at_x(k):
        return {"tm": lax.rem(x + k, SIDE) * SIDE + z}

    def at_z(k):
        return {"tm": x * SIDE + lax.rem(z + k, SIDE)}

    def at_tm(k):
        return {"tm": lax.rem(me + k, n_tm)}

    def at_plane(k):
        kx, ky = k // SIDE, k % SIDE
        return {
            "tm": lax.rem(x + kx, SIDE) * SIDE + z,
            "lib": lax.rem(far_at + ky, SIDE) * near + near_at,
        }

    def at_near(k):
        return {"lib": far_at * near + lax.rem(near_at + k, near)}

    def column(k):
        return lax.rem(z * near + near_at + k, SIDE * near)

    def at_column(k):
        to = column(k)
        return {"tm": x * SIDE + to // near, "lib": far_at * near + lax.rem(to, near)}

    core = lax.rem(near_at, 2)

    def send(src, dst, s, r, to):
        return pltpu.make_async_remote_copy(
            src_ref=src, dst_ref=dst, send_sem=s, recv_sem=r, device_id=to, device_id_type=MESH
        )

    loads = [
        pltpu.make_async_copy(a, b, in_sem.at[n])
        for n, (a, b) in enumerate(
            ((slot_h, slot), (tmpl, blk), (rec_h, rec), (owner_h, owner), (mask_h, mask))
        )
    ]
    for copy in loads:
        copy.start()
    barrier = pltpu.get_barrier_semaphore()
    cousins = [at_near(k) for k in range(1, near)] + [at_plane(k) for k in range(1, SIDE)]
    peers = [at_z(k) for k in range(1, SIDE)] + [at_x(k) for k in range(1, SIDE)] + cousins
    for to in peers:
        pl.semaphore_signal(barrier, inc=1, device_id=to, device_id_type=MESH)

    lane = lax.broadcasted_iota(jnp.int32, (1, LANES), 1)
    acc[...] = jnp.zeros_like(acc)
    used = taps + SHIFTS
    right[:, used:, :] = jnp.zeros((channels, right.shape[1] - used, 2 * LANES), bf)
    g32[pl.ds(rows * channels, 2 * channels), :] = jnp.zeros((2 * channels, LANES), f32)
    for n in (0, 2, 3, 4):
        loads[n].wait()
    half = per_dev // 2
    for ii in range(half):
        for at_core in range(2):

            @pl.when(core == at_core)
            def _():
                a = LANES * (at_core * half + ii)
                recg[me, at_core, ii] = rec[:, a : a + LANES]

    owner_x = [owner[0, r] // SIDE for r in range(2)]
    owner_z = [lax.rem(owner[0, r], SIDE) for r in range(2)]
    loads[1].wait()

    def pick(q, _):
        for r in range(2):
            for cc in range(CHUNK):
                for j in range(SIDE):
                    for h in range(2):
                        own[q, j, 2 * r + h, PER * cc : PER * (cc + 1), :] = blk[
                            slot[0, r], q * CHUNK + cc, (2 * j + h) * PER : (2 * j + h + 1) * PER, :
                        ]
        return 0

    lax.fori_loop(0, chunks, pick, 0)
    pl.semaphore_wait(barrier, len(peers))

    def rec_z(k):
        part = recg.at[me, core]
        return send(part, part, bz_s.at[k - 1], bz_r.at[k - 1], at_z(k))

    def rec_x(k):
        part = recg.at[pl.ds(x * SIDE, SIDE), core]
        return send(part, part, bx_s.at[k - 1], bx_r.at[k - 1], at_x(k))

    def rec_core():
        part = recg.at[:, core]
        to = {"lib": lib + 1 - 2 * core}
        return send(part, part, bc_s, bc_r, to)

    def tmpl_x(q, k):
        return send(
            own.at[q, lax.rem(x + k, SIDE)], rsx.at[q, k - 1], x_s.at[q, k - 1], x_r.at[q, k - 1], at_x(k)
        )

    def tmpl_z(q, k):
        return send(
            cand.at[q, lax.rem(z + k, SIDE)], rsz.at[q, k - 1], z_s.at[q, k - 1], z_r.at[q, k - 1], at_z(k)
        )

    order = (2, 1, 3)

    def start_x(a, b):
        for q in range(a, b):
            for k in order:
                tmpl_x(q, k).start()

    def pass_on(a, b):
        for q in range(a, b):
            for k in order:
                tmpl_x(q, k).wait_recv()
            for i in range(SIDE):
                v = own[q, x, i]
                for k in range(1, SIDE):
                    v = jnp.where(owner_x[i // 2] == lax.rem(x + SIDE - k, SIDE), rsx[q, k - 1, i], v)
                cand[q, i] = v
            for k in order:
                tmpl_z(q, k).start()

    group = 8

    def spread_out(b, _):
        for n in range(group):
            i = b * group + n
            v = recg[i // per_dev, lax.rem(i, per_dev) // half, lax.rem(i, half)].astype(f32)
            g32[pl.ds(pl.multiple_of(i * channels, 8), channels), :] = v
        return 0

    def weigh(b, band):
        n = group * channels
        a = pl.multiple_of(b * n, 8)
        top, rest = [], []
        for k in range(3):
            v = g32[pl.ds(a + channels * k, n), :]
            sq = v * v
            top.append(sq.astype(bf))
            rest.append((sq - top[k].astype(f32)).astype(bf))
        e = jnp.dot(jnp.concatenate(top, axis=1), band, preferred_element_type=f32)
        e = e + jnp.dot(jnp.concatenate(rest, axis=1), band, preferred_element_type=f32)
        wt32[pl.ds(a, n), :] = 1.0 / jnp.sqrt(jnp.maximum(e, jnp.float32(taps / 4)))
        return band

    def windows(b, _):
        c = 2 * b
        raw = [g32[pl.ds(c + n, rows, stride=channels), :] for n in range(2)]
        t0 = jnp.concatenate(raw, axis=0).T
        at = lax.rem(lane, HALF)
        flat = [t0] + [jnp.where(at < HALF - k, pltpu.roll(t0, LANES - k, axis=1), 0.0) for k in (1, 2)]
        turned = jnp.concatenate([pltpu.roll(t, HALF, axis=1) for t in flat], axis=0)
        flat = jnp.concatenate(flat, axis=0)
        g = [
            jnp.where(mask[c + n] != 0, wt32[pl.ds(c + n, rows, stride=channels), :], 0.0) for n in range(2)
        ]
        g = jnp.concatenate(g, axis=0).T
        g_turned = pltpu.roll(g, HALF, axis=1)
        for n, (f, t, gf, gt) in enumerate(((flat, turned, g, g_turned), (turned, flat, g_turned, g))):
            for p in range(2):
                a = 2 * SHIFTS * p
                w = jnp.where(lane < HALF, f[a : a + used], t[a + SHIFTS : a + SHIFTS + used])
                right[c + n, :used, LANES * p : LANES * (p + 1)] = w.astype(bf)
                tile[c + n, p] = jnp.where(lane < HALF, gf[a : a + SHIFTS], gt[a + SHIFTS : a + 2 * SHIFTS])
        return 0

    mine = z // 2
    own_z = jnp.where(mine == 0, owner_z[0], owner_z[1])

    def build(q, _):
        for k in order:
            tmpl_z(q, k).wait_recv()
        v = cand[q, z]
        for k in range(1, SIDE):
            v = jnp.where(own_z == lax.rem(z + SIDE - k, SIDE), rsz[q, k - 1], v)
        wide = v.astype(f32)
        inv = 1.0 / jnp.sqrt(jnp.sum(wide * wide, axis=1, keepdims=True) + 1e-06)
        unit = (wide * inv).astype(bf).astype(f32)
        for cc in range(CHUNK):
            c = q * CHUNK + cc
            u0 = unit[PER * cc : PER * (cc + 1), :LANES]
            u1 = unit[PER * cc : PER * (cc + 1), LANES:]
            for s in range(0, SHIFTS, 2):
                cols = [[], [], []]
                for b in (s, s + 1):
                    r0 = u0 if b == 0 else pltpu.roll(u0, b, axis=1)
                    r1 = u1 if b == 0 else pltpu.roll(u1, b, axis=1)
                    cols[0].append(jnp.where(lane < b, 0.0, r0))
                    cols[1].append(jnp.where(lane < b, r0, r1))
                    cols[2].append(jnp.where(lane < b, r1, 0.0))
                for p in range(3):
                    lhs[c, PER * s : PER * (s + 2), LANES * p : LANES * (p + 1)] = jnp.concatenate(
                        cols[p], axis=0
                    ).astype(bf)
        return 0

    def multiply(q, _):
        corr = [jnp.dot(lhs[q * CHUNK + n], right[q * CHUNK + n], preferred_element_type=f32) for n in range(CHUNK)]
        for p in range(2):
            for s in range(SHIFTS):
                part, cols = slice(PER * s, PER * (s + 1)), slice(LANES * p, LANES * (p + 1))
                v = acc[p, part, :]
                for n in range(CHUNK):
                    v = v + corr[n][part, cols] * tile[q * CHUNK + n, p, s : s + 1, :]
                acc[p, part, :] = v
        return 0

    def both(q, _):
        build(q, 0)
        multiply(q, 0)
        return 0

    def step(a, b):
        for q in range(a, b):
            pass_on(q, q + 1)
            if q + DEPTH < chunks:
                start_x(q + DEPTH, q + DEPTH + 1)

    at_p = lax.broadcasted_iota(jnp.int32, (3 * LANES, LANES), 0)
    at_l = lax.broadcasted_iota(jnp.int32, (3 * LANES, LANES), 1)
    band = jnp.where((at_p >= at_l) & (at_p < at_l + taps), 1.0, 0.0).astype(bf)
    pairs, blocks = channels // 2, rows // group

    for k in order:
        rec_z(k).start()
    start_x(0, DEPTH)
    step(0, 4)
    for k in order:
        rec_z(k).wait_recv()
    for k in order:
        rec_x(k).start()
    step(4, 6)
    build(0, 0)
    step(6, 7)
    build(1, 0)
    for to in cousins:
        pl.semaphore_signal(vouch, inc=1, device_id=to, device_id_type=MESH)
    for k in order:
        rec_x(k).wait_recv()
    rec_core().start()
    step(7, 8)
    lax.fori_loop(2, 4, build, 0)
    step(8, 9)
    rec_core().wait_recv()
    lax.fori_loop(0, blocks, spread_out, 0)
    step(9, 10)
    lax.fori_loop(0, blocks // 2, weigh, band)
    step(10, 11)
    lax.fori_loop(blocks // 2, blocks, weigh, band)
    step(11, 12)
    lax.fori_loop(4, 5, build, 0)
    lax.fori_loop(0, pairs // 2, windows, 0)
    lax.fori_loop(5, 7, build, 0)
    lax.fori_loop(pairs // 2, pairs, windows, 0)
    lax.fori_loop(7, 9, build, 0)
    lax.fori_loop(0, 9, multiply, 0)
    lax.fori_loop(9, chunks, both, 0)

    count = mask[0]
    for c in range(1, channels):
        count = count + mask[c]
    count_f = jnp.maximum(jnp.full((8, LANES), count, jnp.int32).astype(f32), 1.0)
    gain = (jnp.sqrt(jnp.float32(taps)) / jnp.sqrt(count_f))[:1]
    def natural(a, b):
        v = jnp.concatenate([a, pltpu.roll(a, HALF, axis=1), b, pltpu.roll(b, HALF, axis=1)], axis=0)
        return v.T[:rows] * gain

    def template(p, m):
        return acc[p, pl.ds(m, SHIFTS, stride=PER), :]

    top = natural(*(functools.reduce(jnp.maximum, [template(p, m) for m in range(PER)]) for p in range(2)))
    for t in range(SIDE):
        pa_s[t] = top[per_dev * SIDE * t : per_dev * SIDE * (t + 1), :]

    def peak_plane(k):
        return send(pa_s.at[lax.rem(x + k // SIDE, SIDE)], pa_r.at[k - 1], m_s.at[k - 1], m_r.at[k - 1], at_plane(k))

    def peak_column(k):
        return send(pb_s.at[column(k) // near], pb_r.at[k - 1], n_s.at[k - 1], n_r.at[k - 1], at_column(k))

    place = out.at[mine, pl.ds(pl.multiple_of((2 * x + lax.rem(z, 2)) * PER, PER), PER), :]

    def stack_tm(k):
        return send(sbuf.at[lax.rem(me + k, n_tm)], place, o_s.at[k - 1], o_r.at[k - 1], at_tm(k))

    pl.semaphore_wait(vouch, len(cousins))
    for k in range(1, SIDE * SIDE):
        peak_plane(k).start()
    for m in range(PER):
        nt[pl.ds(m, rows, stride=PER), :] = natural(template(0, m), template(1, m))
    for t in range(n_tm):
        for ii in range(per_dev):
            a = (per_dev * t + ii) * PER
            sbuf[t, :, LANES * ii : LANES * (ii + 1)] = nt[a : a + PER, :].astype(bf)
    for k in range(1, n_tm):
        stack_tm(k).start()
    out[mine, pl.ds(pl.multiple_of((2 * x + lax.rem(z, 2)) * PER, PER), PER), :] = sbuf[me]
    peak = pa_s[x]
    for k in range(1, SIDE * SIDE):
        peak_plane(k).wait_recv()
        peak = jnp.maximum(peak, pa_r[k - 1])
    for t in range(SIDE):
        pb_s[t] = peak[per_dev * t : per_dev * (t + 1), :]
    for k in sorted(range(1, SIDE * near), key=lambda k: -min(k, SIDE * near - k)):
        peak_column(k).start()
    peak = pb_s[z]
    for k in range(1, SIDE * near):
        peak_column(k).wait_recv()
        peak = jnp.maximum(peak, pb_r[k - 1])
    best[...] = peak
    for k in range(1, n_tm):
        stack_tm(k).wait_recv()
    for k in order:
        rec_z(k).wait_send()
        rec_x(k).wait_send()
        for q in range(chunks):
            tmpl_x(q, k).wait_send()
            tmpl_z(q, k).wait_send()
    rec_core().wait_send()
    for k in range(1, n_tm):
        stack_tm(k).wait_send()
    for k in range(1, SIDE * SIDE):
        peak_plane(k).wait_send()
    for k in range(1, SIDE * near):
        peak_column(k).wait_send()


def on_device(record, templates, owner, slot, mask):
    channels, samples = record.shape
    block, taps = templates.shape[-2:]
    rounds = owner.shape[1]
    n_tm, n_lib = lax.axis_size("tm"), lax.axis_size("lib")
    chunks = channels // CHUNK
    per_dev = samples // LANES
    rows = n_tm * per_dev
    near = n_lib // SIDE
    vm, bf, f32 = pltpu.VMEM, jnp.bfloat16, jnp.float32
    dma = pltpu.SemaphoreType.DMA
    vmem = pl.BlockSpec(memory_space=pltpu.VMEM)
    hbm = pl.BlockSpec(memory_space=pltpu.MemorySpace.HBM)
    piece = (CHUNK * PER, taps)

    stacks, best = pl.pallas_call(
        functools.partial(kernel, n_tm, n_lib),
        out_shape=(
            jax.ShapeDtypeStruct((rounds, block, samples), bf),
            jax.ShapeDtypeStruct((per_dev, LANES), f32),
        ),
        in_specs=[hbm] * 5,
        out_specs=(vmem, vmem),
        scratch_shapes=[
            vm((channels, samples), bf),
            pltpu.SMEM(owner.shape, jnp.int32),
            pltpu.SMEM(slot.shape, jnp.int32),
            pltpu.SMEM(mask.shape, jnp.int32),
            vm(templates.shape[2:], bf),
            vm((chunks, SIDE, SIDE, *piece), bf),
            vm((chunks, SIDE - 1, SIDE, *piece), bf),
            vm((chunks, SIDE, *piece), bf),
            vm((chunks, SIDE - 1, *piece), bf),
            vm((n_tm, 2, per_dev // 2, channels, LANES), bf),
            vm(((rows + 2) * channels, LANES), f32),
            vm((channels, 3 * LANES, 2 * LANES), bf),
            vm((channels, SHIFTS * PER, 3 * LANES), bf),
            vm((rows * channels, LANES), f32),
            vm((channels, 2, SHIFTS, LANES), f32),
            vm((rows * PER, LANES), f32),
            vm((2, SHIFTS * PER, LANES), f32),
            vm((n_tm, PER, samples), bf),
            vm((SIDE, SIDE * per_dev, LANES), f32),
            vm((SIDE * SIDE - 1, SIDE * per_dev, LANES), f32),
            vm((SIDE, per_dev, LANES), f32),
            vm((SIDE * near - 1, per_dev, LANES), f32),
            dma((5,)),
            dma((3,)), dma((3,)), dma((3,)), dma((3,)),
            dma((chunks, 3)), dma((chunks, 3)), dma((chunks, 3)), dma((chunks, 3)),
            dma((n_tm - 1,)), dma((n_tm - 1,)), dma((SIDE * SIDE - 1,)), dma((SIDE * SIDE - 1,)),
            dma((SIDE * near - 1,)), dma((SIDE * near - 1,)), dma, dma, pltpu.SemaphoreType.REGULAR,
        ],
        compiler_params=pltpu.CompilerParams(
            collective_id=0, has_side_effects=True, vmem_limit_bytes=48 << 20
        ),
        name="match",
    )(*(pltpu.with_memory_space_constraint(a, pltpu.MemorySpace.HBM) for a in (record, templates[0, 0], owner, slot, mask)))
    return stacks[None], best.reshape(samples)


def solution(mesh):
    placed = (
        P(None, "tm"),
        P("lib", "tm", None, None, None, None),
        P("lib", None),
        P("lib", None),
        P(),
    )
    return jax.shard_map(
        on_device,
        mesh=mesh,
        in_specs=placed,
        out_specs=(P("lib", None, None, "tm"), P("tm")),
        check_vma=False,
    )
```

```python
import functools

import jax
import jax.numpy as jnp
from jax import lax
from jax.experimental import pallas as pl
from jax.experimental.pallas import tpu as pltpu
from jax.sharding import PartitionSpec as P

MESH = pl.DeviceIdType.MESH
LANES = 128
HALF = LANES // 2
SHIFTS = 32
PER = 8
SIDE = 4
CHUNK = 2
DEPTH = 5
AHEAD = 6


def kernel(
    n_tm, n_lib, rec_h, tmpl, owner_h, slot_h, mask_h, out, best,
    rec, owner, slot, mask, blk, own, rsx, cand, rsz, recg, g32, parts, right, lhs, wt32, tile, nt, acc,
    sbuf, pa_s, pa_r, pb_s, pb_r,
    in_sem, bz_s, bz_r, bx_s, bx_r, x_s, x_r, z_s, z_r, o_s, o_r, m_s, m_r, n_s, n_r, bc_s, bc_r, vouch,
):
    slots, channels, block, taps = tmpl.shape
    samples = rec.shape[1]
    me = lax.axis_index("tm")
    lib = lax.axis_index("lib")
    x, z = me // SIDE, lax.rem(me, SIDE)
    near = n_lib // SIDE
    far_at, near_at = lib // near, lax.rem(lib, near)
    chunks = channels // CHUNK
    per_dev = samples // LANES
    rows = n_tm * per_dev
    f32, bf = jnp.float32, jnp.bfloat16

    def at_x(k):
        return {"tm": lax.rem(x + k, SIDE) * SIDE + z}

    def at_z(k):
        return {"tm": x * SIDE + lax.rem(z + k, SIDE)}

    def at_tm(k):
        return {"tm": lax.rem(me + k, n_tm)}

    def at_plane(k):
        kx, ky = k // SIDE, k % SIDE
        return {
            "tm": lax.rem(x + kx, SIDE) * SIDE + z,
            "lib": lax.rem(far_at + ky, SIDE) * near + near_at,
        }

    def at_near(k):
        return {"lib": far_at * near + lax.rem(near_at + k, near)}

    def column(k):
        return lax.rem(z * near + near_at + k, SIDE * near)

    def at_column(k):
        to = column(k)
        return {"tm": x * SIDE + to // near, "lib": far_at * near + lax.rem(to, near)}

    core = lax.rem(near_at, 2)

    def send(src, dst, s, r, to):
        return pltpu.make_async_remote_copy(
            src_ref=src, dst_ref=dst, send_sem=s, recv_sem=r, device_id=to, device_id_type=MESH
        )

    loads = [
        pltpu.make_async_copy(a, b, in_sem.at[n])
        for n, (a, b) in enumerate(
            ((slot_h, slot), (tmpl, blk), (rec_h, rec), (owner_h, owner), (mask_h, mask))
        )
    ]
    for copy in loads:
        copy.start()
    barrier = pltpu.get_barrier_semaphore()
    cousins = [at_near(k) for k in range(1, near)] + [at_plane(k) for k in range(1, SIDE)]
    peers = [at_z(k) for k in range(1, SIDE)] + [at_x(k) for k in range(1, SIDE)] + cousins
    for to in peers:
        pl.semaphore_signal(barrier, inc=1, device_id=to, device_id_type=MESH)

    lane = lax.broadcasted_iota(jnp.int32, (1, LANES), 1)
    acc[...] = jnp.zeros_like(acc)
    used = taps + SHIFTS
    right[:, used:, :] = jnp.zeros((channels, right.shape[1] - used, 2 * LANES), bf)
    g32[pl.ds(rows * channels, 2 * channels), :] = jnp.zeros((2 * channels, LANES), f32)
    parts[:, pl.ds(rows, 2)] = jnp.zeros((2, 2, channels, LANES), bf)
    for n in (0, 2, 3, 4):
        loads[n].wait()
    half = per_dev // 2
    for ii in range(half):
        for at_core in range(2):

            @pl.when(core == at_core)
            def _():
                a = LANES * (at_core * half + ii)
                recg[me, at_core, ii] = rec[:, a : a + LANES]

    owner_x = [owner[0, r] // SIDE for r in range(2)]
    owner_z = [lax.rem(owner[0, r], SIDE) for r in range(2)]
    loads[1].wait()

    def pick(q, _):
        for r in range(2):
            for cc in range(CHUNK):
                for j in range(SIDE):
                    for h in range(2):
                        own[q, j, 2 * r + h, PER * cc : PER * (cc + 1), :] = blk[
                            slot[0, r], q * CHUNK + cc, (2 * j + h) * PER : (2 * j + h + 1) * PER, :
                        ]
        return 0

    lax.fori_loop(0, chunks, pick, 0)
    pl.semaphore_wait(barrier, len(peers))

    def rec_z(k):
        part = recg.at[me, core]
        return send(part, part, bz_s.at[k - 1], bz_r.at[k - 1], at_z(k))

    def rec_x(k):
        part = recg.at[pl.ds(x * SIDE, SIDE), core]
        return send(part, part, bx_s.at[k - 1], bx_r.at[k - 1], at_x(k))

    def rec_core():
        part = recg.at[:, core]
        to = {"lib": lib + 1 - 2 * core}
        return send(part, part, bc_s, bc_r, to)

    def tmpl_x(q, k):
        return send(
            own.at[q, lax.rem(x + k, SIDE)], rsx.at[q, k - 1], x_s.at[q, k - 1], x_r.at[q, k - 1], at_x(k)
        )

    def tmpl_z(q, k):
        return send(
            cand.at[q, lax.rem(z + k, SIDE)], rsz.at[q, k - 1], z_s.at[q, k - 1], z_r.at[q, k - 1], at_z(k)
        )

    order = (2, 1, 3)

    def start_x(a, b):
        for q in range(a, b):
            for k in order:
                tmpl_x(q, k).start()

    def pass_on(a, b):
        for q in range(a, b):
            for k in order:
                tmpl_x(q, k).wait_recv()
            for i in range(SIDE):
                v = own[q, x, i]
                for k in range(1, SIDE):
                    v = jnp.where(owner_x[i // 2] == lax.rem(x + SIDE - k, SIDE), rsx[q, k - 1, i], v)
                cand[q, i] = v
            for k in order:
                tmpl_z(q, k).start()

    group = 8

    def spread_out(b, _):
        for n in range(group):
            i = b * group + n
            v = recg[i // per_dev, lax.rem(i, per_dev) // half, lax.rem(i, half)].astype(f32)
            sq = v * v
            high = sq.astype(bf)
            g32[pl.ds(pl.multiple_of(i * channels, 8), channels), :] = v
            parts[0, i] = high
            parts[1, i] = (sq - high.astype(f32)).astype(bf)
        return 0

    def weigh(b, band):
        n = group * channels
        a = pl.multiple_of(b * n, 8)
        e = None
        for h in range(2):
            v = [parts[h, pl.ds(b * group + k, group)].reshape(n, LANES) for k in range(3)]
            d = jnp.dot(jnp.concatenate(v, axis=1), band, preferred_element_type=f32)
            e = d if h == 0 else e + d
        wt32[pl.ds(a, n), :] = 1.0 / jnp.sqrt(jnp.maximum(e, jnp.float32(taps / 4)))
        return band

    def windows(b, _):
        c = 2 * b
        raw = [g32[pl.ds(c + n, rows, stride=channels), :] for n in range(2)]
        t0 = jnp.concatenate(raw, axis=0).T
        at = lax.rem(lane, HALF)
        flat = [t0] + [jnp.where(at < HALF - k, pltpu.roll(t0, LANES - k, axis=1), 0.0) for k in (1, 2)]
        turned = jnp.concatenate([pltpu.roll(t, HALF, axis=1) for t in flat], axis=0)
        flat = jnp.concatenate(flat, axis=0)
        g = [
            jnp.where(mask[c + n] != 0, wt32[pl.ds(c + n, rows, stride=channels), :], 0.0) for n in range(2)
        ]
        g = jnp.concatenate(g, axis=0).T
        g_turned = pltpu.roll(g, HALF, axis=1)
        for n, (f, t, gf, gt) in enumerate(((flat, turned, g, g_turned), (turned, flat, g_turned, g))):
            for p in range(2):
                a = 2 * SHIFTS * p
                w = jnp.where(lane < HALF, f[a : a + used], t[a + SHIFTS : a + SHIFTS + used])
                right[c + n, :used, LANES * p : LANES * (p + 1)] = w.astype(bf)
                tile[c + n, p] = jnp.where(lane < HALF, gf[a : a + SHIFTS], gt[a + SHIFTS : a + 2 * SHIFTS])
        return 0

    mine = z // 2
    own_z = jnp.where(mine == 0, owner_z[0], owner_z[1])

    def build(q, _):
        for k in order:
            tmpl_z(q, k).wait_recv()
        v = cand[q, z]
        for k in range(1, SIDE):
            v = jnp.where(own_z == lax.rem(z + SIDE - k, SIDE), rsz[q, k - 1], v)
        wide = v.astype(f32)
        inv = 1.0 / jnp.sqrt(jnp.sum(wide * wide, axis=1, keepdims=True) + 1e-06)
        unit = (wide * inv).astype(bf).astype(f32)
        for cc in range(CHUNK):
            c = q * CHUNK + cc
            u0 = unit[PER * cc : PER * (cc + 1), :LANES]
            u1 = unit[PER * cc : PER * (cc + 1), LANES:]
            for s in range(0, SHIFTS, 2):
                cols = [[], [], []]
                for b in (s, s + 1):
                    r0 = u0 if b == 0 else pltpu.roll(u0, b, axis=1)
                    r1 = u1 if b == 0 else pltpu.roll(u1, b, axis=1)
                    cols[0].append(jnp.where(lane < b, 0.0, r0))
                    cols[1].append(jnp.where(lane < b, r0, r1))
                    cols[2].append(jnp.where(lane < b, r1, 0.0))
                for p in range(3):
                    lhs[c, PER * s : PER * (s + 2), LANES * p : LANES * (p + 1)] = jnp.concatenate(
                        cols[p], axis=0
                    ).astype(bf)
        return 0

    def multiply(q, _):
        corr = [jnp.dot(lhs[q * CHUNK + n], right[q * CHUNK + n], preferred_element_type=f32) for n in range(CHUNK)]
        for p in range(2):
            for s in range(SHIFTS):
                part, cols = slice(PER * s, PER * (s + 1)), slice(LANES * p, LANES * (p + 1))
                v = acc[p, part, :]
                for n in range(CHUNK):
                    v = v + corr[n][part, cols] * tile[q * CHUNK + n, p, s : s + 1, :]
                acc[p, part, :] = v
        return 0

    def both(q, _):
        build(q, 0)
        multiply(q, 0)
        return 0

    def step(a, b):
        for q in range(a, b):
            pass_on(q, q + 1)
            if q + DEPTH < chunks:
                start_x(q + DEPTH, q + DEPTH + 1)

    at_p = lax.broadcasted_iota(jnp.int32, (3 * LANES, LANES), 0)
    at_l = lax.broadcasted_iota(jnp.int32, (3 * LANES, LANES), 1)
    band = jnp.where((at_p >= at_l) & (at_p < at_l + taps), 1.0, 0.0).astype(bf)
    pairs, blocks = channels // 2, rows // group

    for k in order:
        rec_z(k).start()
    start_x(0, AHEAD)
    pass_on(0, 3)
    for k in order:
        rec_z(k).wait_recv()
    for k in order:
        rec_x(k).start()
    start_x(AHEAD, 8)
    step(3, 6)
    build(0, 0)
    for to in cousins:
        pl.semaphore_signal(vouch, inc=1, device_id=to, device_id_type=MESH)
    for k in order:
        rec_x(k).wait_recv()
    rec_core().start()
    step(6, 7)
    build(1, 0)
    step(7, 8)
    rec_core().wait_recv()
    lax.fori_loop(0, blocks, spread_out, 0)
    step(8, 9)
    build(2, 0)
    lax.fori_loop(0, blocks // 4, weigh, band)
    step(9, 10)
    build(3, 0)
    lax.fori_loop(blocks // 4, blocks // 2, weigh, band)
    step(10, 11)
    lax.fori_loop(blocks // 2, blocks, weigh, band)
    step(11, 12)
    lax.fori_loop(0, pairs // 2, windows, 0)
    lax.fori_loop(4, 7, build, 0)
    lax.fori_loop(pairs // 2, pairs, windows, 0)
    build(7, 0)
    lax.fori_loop(0, 8, multiply, 0)
    lax.fori_loop(8, chunks, both, 0)

    count = mask[0]
    for c in range(1, channels):
        count = count + mask[c]
    count_f = jnp.maximum(jnp.full((8, LANES), count, jnp.int32).astype(f32), 1.0)
    gain = (jnp.sqrt(jnp.float32(taps)) / jnp.sqrt(count_f))[:1]
    def natural(a, b):
        v = jnp.concatenate([a, pltpu.roll(a, HALF, axis=1), b, pltpu.roll(b, HALF, axis=1)], axis=0)
        return v.T[:rows] * gain

    def template(p, m):
        return acc[p, pl.ds(m, SHIFTS, stride=PER), :]

    top = natural(*(functools.reduce(jnp.maximum, [template(p, m) for m in range(PER)]) for p in range(2)))
    for t in range(SIDE):
        pa_s[t] = top[per_dev * SIDE * t : per_dev * SIDE * (t + 1), :]

    def peak_plane(k):
        return send(pa_s.at[lax.rem(x + k // SIDE, SIDE)], pa_r.at[k - 1], m_s.at[k - 1], m_r.at[k - 1], at_plane(k))

    def peak_column(k):
        return send(pb_s.at[column(k) // near], pb_r.at[k - 1], n_s.at[k - 1], n_r.at[k - 1], at_column(k))

    place = out.at[mine, pl.ds(pl.multiple_of((2 * x + lax.rem(z, 2)) * PER, PER), PER), :]

    def stack_tm(k):
        return send(sbuf.at[lax.rem(me + k, n_tm)], place, o_s.at[k - 1], o_r.at[k - 1], at_tm(k))

    pl.semaphore_wait(vouch, len(cousins))
    for k in range(1, SIDE * SIDE):
        peak_plane(k).start()
    for m in range(PER):
        nt[pl.ds(m, rows, stride=PER), :] = natural(template(0, m), template(1, m))
    for t in range(n_tm):
        for ii in range(per_dev):
            a = (per_dev * t + ii) * PER
            sbuf[t, :, LANES * ii : LANES * (ii + 1)] = nt[a : a + PER, :].astype(bf)
    for k in range(1, n_tm):
        stack_tm(k).start()
    out[mine, pl.ds(pl.multiple_of((2 * x + lax.rem(z, 2)) * PER, PER), PER), :] = sbuf[me]
    peak = pa_s[x]
    for k in range(1, SIDE * SIDE):
        peak_plane(k).wait_recv()
        peak = jnp.maximum(peak, pa_r[k - 1])
    for t in range(SIDE):
        pb_s[t] = peak[per_dev * t : per_dev * (t + 1), :]
    for k in sorted(range(1, SIDE * near), key=lambda k: -min(k, SIDE * near - k)):
        peak_column(k).start()
    peak = pb_s[z]
    for k in range(1, SIDE * near):
        peak_column(k).wait_recv()
        peak = jnp.maximum(peak, pb_r[k - 1])
    best[...] = peak
    for k in range(1, n_tm):
        stack_tm(k).wait_recv()
    for k in order:
        rec_z(k).wait_send()
        rec_x(k).wait_send()
        for q in range(chunks):
            tmpl_x(q, k).wait_send()
            tmpl_z(q, k).wait_send()
    rec_core().wait_send()
    for k in range(1, n_tm):
        stack_tm(k).wait_send()
    for k in range(1, SIDE * SIDE):
        peak_plane(k).wait_send()
    for k in range(1, SIDE * near):
        peak_column(k).wait_send()


def on_device(record, templates, owner, slot, mask):
    channels, samples = record.shape
    block, taps = templates.shape[-2:]
    rounds = owner.shape[1]
    n_tm, n_lib = lax.axis_size("tm"), lax.axis_size("lib")
    chunks = channels // CHUNK
    per_dev = samples // LANES
    rows = n_tm * per_dev
    near = n_lib // SIDE
    vm, bf, f32 = pltpu.VMEM, jnp.bfloat16, jnp.float32
    dma = pltpu.SemaphoreType.DMA
    vmem = pl.BlockSpec(memory_space=pltpu.VMEM)
    hbm = pl.BlockSpec(memory_space=pltpu.MemorySpace.HBM)
    piece = (CHUNK * PER, taps)

    stacks, best = pl.pallas_call(
        functools.partial(kernel, n_tm, n_lib),
        out_shape=(
            jax.ShapeDtypeStruct((rounds, block, samples), bf),
            jax.ShapeDtypeStruct((per_dev, LANES), f32),
        ),
        in_specs=[hbm] * 5,
        out_specs=(vmem, vmem),
        scratch_shapes=[
            vm((channels, samples), bf),
            pltpu.SMEM(owner.shape, jnp.int32),
            pltpu.SMEM(slot.shape, jnp.int32),
            pltpu.SMEM(mask.shape, jnp.int32),
            vm(templates.shape[2:], bf),
            vm((chunks, SIDE, SIDE, *piece), bf),
            vm((chunks, SIDE - 1, SIDE, *piece), bf),
            vm((chunks, SIDE, *piece), bf),
            vm((chunks, SIDE - 1, *piece), bf),
            vm((n_tm, 2, per_dev // 2, channels, LANES), bf),
            vm(((rows + 2) * channels, LANES), f32),
            vm((2, rows + 2, channels, LANES), bf),
            vm((channels, 3 * LANES, 2 * LANES), bf),
            vm((channels, SHIFTS * PER, 3 * LANES), bf),
            vm((rows * channels, LANES), f32),
            vm((channels, 2, SHIFTS, LANES), f32),
            vm((rows * PER, LANES), f32),
            vm((2, SHIFTS * PER, LANES), f32),
            vm((n_tm, PER, samples), bf),
            vm((SIDE, SIDE * per_dev, LANES), f32),
            vm((SIDE * SIDE - 1, SIDE * per_dev, LANES), f32),
            vm((SIDE, per_dev, LANES), f32),
            vm((SIDE * near - 1, per_dev, LANES), f32),
            dma((5,)),
            dma((3,)), dma((3,)), dma((3,)), dma((3,)),
            dma((chunks, 3)), dma((chunks, 3)), dma((chunks, 3)), dma((chunks, 3)),
            dma((n_tm - 1,)), dma((n_tm - 1,)), dma((SIDE * SIDE - 1,)), dma((SIDE * SIDE - 1,)),
            dma((SIDE * near - 1,)), dma((SIDE * near - 1,)), dma, dma, pltpu.SemaphoreType.REGULAR,
        ],
        compiler_params=pltpu.CompilerParams(
            collective_id=0, has_side_effects=True, vmem_limit_bytes=48 << 20
        ),
        name="match",
    )(*(pltpu.with_memory_space_constraint(a, pltpu.MemorySpace.HBM) for a in (record, templates[0, 0], owner, slot, mask)))
    return stacks[None], best.reshape(samples)


def solution(mesh):
    placed = (
        P(None, "tm"),
        P("lib", "tm", None, None, None, None),
        P("lib", None),
        P("lib", None),
        P(),
    )
    return jax.shard_map(
        on_device,
        mesh=mesh,
        in_specs=placed,
        out_specs=(P("lib", None, None, "tm"), P("tm")),
        check_vma=False,
    )
```

```python
import functools

import jax
import jax.numpy as jnp
from jax import lax
from jax.experimental import pallas as pl
from jax.experimental.pallas import tpu as pltpu
from jax.sharding import PartitionSpec as P

MESH = pl.DeviceIdType.MESH
LANES = 128
HALF = LANES // 2
SHIFTS = 32
PER = 8
SIDE = 4
CHUNK = 2
DEPTH = 5
AHEAD = 6


def kernel(
    n_tm, n_lib, rec_h, tmpl, owner_h, slot_h, mask_h, out, best,
    rec, owner, slot, mask, blk, own, rsx, cand, rsz, recg, g32, parts, right, lhs, wt32, tile, nt, acc,
    sbuf, pa_s, pa_r, pb_s, pb_r,
    in_sem, bz_s, bz_r, bx_s, bx_r, x_s, x_r, z_s, z_r, o_s, o_r, m_s, m_r, n_s, n_r, bc_s, bc_r, vouch,
):
    slots, channels, block, taps = tmpl.shape
    samples = rec.shape[1]
    me = lax.axis_index("tm")
    lib = lax.axis_index("lib")
    x, z = me // SIDE, lax.rem(me, SIDE)
    near = n_lib // SIDE
    far_at, near_at = lib // near, lax.rem(lib, near)
    chunks = channels // CHUNK
    per_dev = samples // LANES
    rows = n_tm * per_dev
    f32, bf = jnp.float32, jnp.bfloat16

    def at_x(k):
        return {"tm": lax.rem(x + k, SIDE) * SIDE + z}

    def at_z(k):
        return {"tm": x * SIDE + lax.rem(z + k, SIDE)}

    def at_tm(k):
        return {"tm": lax.rem(me + k, n_tm)}

    def at_plane(k):
        kx, ky = k // SIDE, k % SIDE
        return {
            "tm": lax.rem(x + kx, SIDE) * SIDE + z,
            "lib": lax.rem(far_at + ky, SIDE) * near + near_at,
        }

    def at_near(k):
        return {"lib": far_at * near + lax.rem(near_at + k, near)}

    def column(k):
        return lax.rem(z * near + near_at + k, SIDE * near)

    def at_column(k):
        to = column(k)
        return {"tm": x * SIDE + to // near, "lib": far_at * near + lax.rem(to, near)}

    core = lax.rem(near_at, 2)

    def send(src, dst, s, r, to):
        return pltpu.make_async_remote_copy(
            src_ref=src, dst_ref=dst, send_sem=s, recv_sem=r, device_id=to, device_id_type=MESH
        )

    loads = [
        pltpu.make_async_copy(a, b, in_sem.at[n])
        for n, (a, b) in enumerate(
            ((slot_h, slot), (tmpl, blk), (rec_h, rec), (owner_h, owner), (mask_h, mask))
        )
    ]
    for copy in loads:
        copy.start()
    barrier = pltpu.get_barrier_semaphore()
    cousins = [at_near(k) for k in range(1, near)] + [at_plane(k) for k in range(1, SIDE)]
    peers = [at_z(k) for k in range(1, SIDE)] + [at_x(k) for k in range(1, SIDE)] + cousins
    for to in peers:
        pl.semaphore_signal(barrier, inc=1, device_id=to, device_id_type=MESH)

    lane = lax.broadcasted_iota(jnp.int32, (1, LANES), 1)
    acc[...] = jnp.zeros_like(acc)
    used = taps + SHIFTS
    right[:, used:, :] = jnp.zeros((channels, right.shape[1] - used, 2 * LANES), bf)
    g32[pl.ds(rows * channels, 2 * channels), :] = jnp.zeros((2 * channels, LANES), f32)
    parts[:, pl.ds(rows, 2)] = jnp.zeros((2, 2, channels, LANES), bf)
    for n in (0, 2, 3, 4):
        loads[n].wait()
    half = per_dev // 2
    for ii in range(half):
        for at_core in range(2):

            @pl.when(core == at_core)
            def _():
                a = LANES * (at_core * half + ii)
                recg[me, at_core, ii] = rec[:, a : a + LANES]

    owner_x = [owner[0, r] // SIDE for r in range(2)]
    owner_z = [lax.rem(owner[0, r], SIDE) for r in range(2)]
    loads[1].wait()

    def pick(q, _):
        for r in range(2):
            for cc in range(CHUNK):
                for j in range(SIDE):
                    for h in range(2):
                        own[q, j, 2 * r + h, PER * cc : PER * (cc + 1), :] = blk[
                            slot[0, r], q * CHUNK + cc, (2 * j + h) * PER : (2 * j + h + 1) * PER, :
                        ]
        return 0

    lax.fori_loop(0, chunks, pick, 0)
    pl.semaphore_wait(barrier, len(peers))

    def rec_z(k):
        part = recg.at[me, core]
        return send(part, part, bz_s.at[k - 1], bz_r.at[k - 1], at_z(k))

    def rec_x(k):
        part = recg.at[pl.ds(x * SIDE, SIDE), core]
        return send(part, part, bx_s.at[k - 1], bx_r.at[k - 1], at_x(k))

    def rec_core():
        part = recg.at[:, core]
        to = {"lib": lib + 1 - 2 * core}
        return send(part, part, bc_s, bc_r, to)

    def tmpl_x(q, k):
        return send(
            own.at[q, lax.rem(x + k, SIDE)], rsx.at[q, k - 1], x_s.at[q, k - 1], x_r.at[q, k - 1], at_x(k)
        )

    def tmpl_z(q, k):
        return send(
            cand.at[q, lax.rem(z + k, SIDE)], rsz.at[q, k - 1], z_s.at[q, k - 1], z_r.at[q, k - 1], at_z(k)
        )

    order = (2, 1, 3)

    def start_x(a, b):
        for q in range(a, b):
            for k in order:
                tmpl_x(q, k).start()

    def pass_on(a, b):
        for q in range(a, b):
            for k in order:
                tmpl_x(q, k).wait_recv()
            for i in range(SIDE):
                v = own[q, x, i]
                for k in range(1, SIDE):
                    v = jnp.where(owner_x[i // 2] == lax.rem(x + SIDE - k, SIDE), rsx[q, k - 1, i], v)
                cand[q, i] = v
            for k in order:
                tmpl_z(q, k).start()

    group = 8

    def spread_out(b, _):
        for n in range(group):
            i = b * group + n
            v = recg[i // per_dev, lax.rem(i, per_dev) // half, lax.rem(i, half)].astype(f32)
            sq = v * v
            high = sq.astype(bf)
            g32[pl.ds(pl.multiple_of(i * channels, 8), channels), :] = v
            parts[0, i] = high
            parts[1, i] = (sq - high.astype(f32)).astype(bf)
        return 0

    def weigh(b, band):
        n = group * channels
        a = pl.multiple_of(b * n, 8)
        e = None
        for h in range(2):
            v = [parts[h, pl.ds(b * group + k, group)].reshape(n, LANES) for k in range(3)]
            d = jnp.dot(jnp.concatenate(v, axis=1), band, preferred_element_type=f32)
            e = d if h == 0 else e + d
        wt32[pl.ds(a, n), :] = 1.0 / jnp.sqrt(jnp.maximum(e, jnp.float32(taps / 4)))
        return band

    def windows(b, _):
        c = 2 * b
        raw = [g32[pl.ds(c + n, rows, stride=channels), :] for n in range(2)]
        t0 = jnp.concatenate(raw, axis=0).T
        at = lax.rem(lane, HALF)
        flat = [t0] + [jnp.where(at < HALF - k, pltpu.roll(t0, LANES - k, axis=1), 0.0) for k in (1, 2)]
        turned = jnp.concatenate([pltpu.roll(t, HALF, axis=1) for t in flat], axis=0)
        flat = jnp.concatenate(flat, axis=0)
        g = [
            jnp.where(mask[c + n] != 0, wt32[pl.ds(c + n, rows, stride=channels), :], 0.0) for n in range(2)
        ]
        g = jnp.concatenate(g, axis=0).T
        g_turned = pltpu.roll(g, HALF, axis=1)
        for n, (f, t, gf, gt) in enumerate(((flat, turned, g, g_turned), (turned, flat, g_turned, g))):
            for p in range(2):
                a = 2 * SHIFTS * p
                w = jnp.where(lane < HALF, f[a : a + used], t[a + SHIFTS : a + SHIFTS + used])
                right[c + n, :used, LANES * p : LANES * (p + 1)] = w.astype(bf)
                tile[c + n, p] = jnp.where(lane < HALF, gf[a : a + SHIFTS], gt[a + SHIFTS : a + 2 * SHIFTS])
        return 0

    mine = z // 2
    own_z = jnp.where(mine == 0, owner_z[0], owner_z[1])

    def build(q, _):
        for k in order:
            tmpl_z(q, k).wait_recv()
        v = cand[q, z]
        for k in range(1, SIDE):
            v = jnp.where(own_z == lax.rem(z + SIDE - k, SIDE), rsz[q, k - 1], v)
        wide = v.astype(f32)
        inv = 1.0 / jnp.sqrt(jnp.sum(wide * wide, axis=1, keepdims=True) + 1e-06)
        unit = (wide * inv).astype(bf).astype(f32)
        for cc in range(CHUNK):
            c = q * CHUNK + cc
            u0 = unit[PER * cc : PER * (cc + 1), :LANES]
            u1 = unit[PER * cc : PER * (cc + 1), LANES:]
            for s in range(0, SHIFTS, 2):
                cols = [[], [], []]
                for b in (s, s + 1):
                    r0 = u0 if b == 0 else pltpu.roll(u0, b, axis=1)
                    r1 = u1 if b == 0 else pltpu.roll(u1, b, axis=1)
                    cols[0].append(jnp.where(lane < b, 0.0, r0))
                    cols[1].append(jnp.where(lane < b, r0, r1))
                    cols[2].append(jnp.where(lane < b, r1, 0.0))
                for p in range(3):
                    lhs[c, PER * s : PER * (s + 2), LANES * p : LANES * (p + 1)] = jnp.concatenate(
                        cols[p], axis=0
                    ).astype(bf)
        return 0

    def multiply(q, _):
        corr = [jnp.dot(lhs[q * CHUNK + n], right[q * CHUNK + n], preferred_element_type=f32) for n in range(CHUNK)]
        for p in range(2):
            for s in range(SHIFTS):
                part, cols = slice(PER * s, PER * (s + 1)), slice(LANES * p, LANES * (p + 1))
                v = acc[p, part, :]
                for n in range(CHUNK):
                    v = v + corr[n][part, cols] * tile[q * CHUNK + n, p, s : s + 1, :]
                acc[p, part, :] = v
        return 0

    def both(q, _):
        build(q, 0)
        multiply(q, 0)
        return 0

    def step(a, b):
        for q in range(a, b):
            pass_on(q, q + 1)
            if q + DEPTH < chunks:
                start_x(q + DEPTH, q + DEPTH + 1)

    at_p = lax.broadcasted_iota(jnp.int32, (3 * LANES, LANES), 0)
    at_l = lax.broadcasted_iota(jnp.int32, (3 * LANES, LANES), 1)
    band = jnp.where((at_p >= at_l) & (at_p < at_l + taps), 1.0, 0.0).astype(bf)
    pairs, blocks = channels // 2, rows // group

    for k in order:
        rec_z(k).start()
    start_x(0, AHEAD)
    pass_on(0, 3)
    for k in order:
        rec_z(k).wait_recv()
    for k in order:
        rec_x(k).start()
    start_x(AHEAD, 8)
    step(3, 6)
    build(0, 0)
    for to in cousins:
        pl.semaphore_signal(vouch, inc=1, device_id=to, device_id_type=MESH)
    for k in order:
        rec_x(k).wait_recv()
    rec_core().start()
    step(6, 7)
    build(1, 0)
    step(7, 8)
    rec_core().wait_recv()
    lax.fori_loop(0, blocks, spread_out, 0)
    step(8, 9)
    build(2, 0)
    lax.fori_loop(0, blocks // 4, weigh, band)
    step(9, 10)
    build(3, 0)
    lax.fori_loop(blocks // 4, blocks // 2, weigh, band)
    step(10, 11)
    lax.fori_loop(blocks // 2, blocks, weigh, band)
    step(11, 12)
    lax.fori_loop(0, pairs // 2, windows, 0)
    lax.fori_loop(4, 7, build, 0)
    lax.fori_loop(pairs // 2, pairs, windows, 0)
    build(7, 0)
    lax.fori_loop(0, 8, multiply, 0)
    lax.fori_loop(8, chunks, both, 0)

    count = mask[0]
    for c in range(1, channels):
        count = count + mask[c]
    count_f = jnp.maximum(jnp.full((8, LANES), count, jnp.int32).astype(f32), 1.0)
    gain = (jnp.sqrt(jnp.float32(taps)) / jnp.sqrt(count_f))[:1]
    def natural(a, b):
        v = jnp.concatenate([a, pltpu.roll(a, HALF, axis=1), b, pltpu.roll(b, HALF, axis=1)], axis=0)
        return v.T[:rows] * gain

    def template(p, m):
        return acc[p, pl.ds(m, SHIFTS, stride=PER), :]

    top = natural(*(functools.reduce(jnp.maximum, [template(p, m) for m in range(PER)]) for p in range(2)))
    for t in range(SIDE):
        pa_s[t] = top[per_dev * SIDE * t : per_dev * SIDE * (t + 1), :]

    def peak_plane(k):
        return send(pa_s.at[lax.rem(x + k // SIDE, SIDE)], pa_r.at[k - 1], m_s.at[k - 1], m_r.at[k - 1], at_plane(k))

    def peak_column(k):
        return send(pb_s.at[column(k) // near], pb_r.at[k - 1], n_s.at[k - 1], n_r.at[k - 1], at_column(k))

    place = out.at[mine, pl.ds(pl.multiple_of((2 * x + lax.rem(z, 2)) * PER, PER), PER), :]

    def stack_tm(k):
        return send(sbuf.at[lax.rem(me + k, n_tm)], place, o_s.at[k - 1], o_r.at[k - 1], at_tm(k))

    pl.semaphore_wait(vouch, len(cousins))
    def hops(k):
        return sum(min(n, SIDE - n) for n in (k // SIDE, k % SIDE))

    for k in sorted(range(1, SIDE * SIDE), key=lambda k: -hops(k)):
        peak_plane(k).start()
    for m in range(PER):
        nt[pl.ds(m, rows, stride=PER), :] = natural(template(0, m), template(1, m))
    for t in range(n_tm):
        for ii in range(per_dev):
            a = (per_dev * t + ii) * PER
            sbuf[t, :, LANES * ii : LANES * (ii + 1)] = nt[a : a + PER, :].astype(bf)
    for k in range(1, n_tm):
        stack_tm(k).start()
    out[mine, pl.ds(pl.multiple_of((2 * x + lax.rem(z, 2)) * PER, PER), PER), :] = sbuf[me]
    peak = pa_s[x]
    for k in range(1, SIDE * SIDE):
        peak_plane(k).wait_recv()
        peak = jnp.maximum(peak, pa_r[k - 1])
    for t in range(SIDE):
        pb_s[t] = peak[per_dev * t : per_dev * (t + 1), :]
    for k in sorted(range(1, SIDE * near), key=lambda k: -min(k, SIDE * near - k)):
        peak_column(k).start()
    peak = pb_s[z]
    for k in range(1, SIDE * near):
        peak_column(k).wait_recv()
        peak = jnp.maximum(peak, pb_r[k - 1])
    best[...] = peak
    for k in range(1, n_tm):
        stack_tm(k).wait_recv()
    for k in order:
        rec_z(k).wait_send()
        rec_x(k).wait_send()
        for q in range(chunks):
            tmpl_x(q, k).wait_send()
            tmpl_z(q, k).wait_send()
    rec_core().wait_send()
    for k in range(1, n_tm):
        stack_tm(k).wait_send()
    for k in range(1, SIDE * SIDE):
        peak_plane(k).wait_send()
    for k in range(1, SIDE * near):
        peak_column(k).wait_send()


def on_device(record, templates, owner, slot, mask):
    channels, samples = record.shape
    block, taps = templates.shape[-2:]
    rounds = owner.shape[1]
    n_tm, n_lib = lax.axis_size("tm"), lax.axis_size("lib")
    chunks = channels // CHUNK
    per_dev = samples // LANES
    rows = n_tm * per_dev
    near = n_lib // SIDE
    vm, bf, f32 = pltpu.VMEM, jnp.bfloat16, jnp.float32
    dma = pltpu.SemaphoreType.DMA
    vmem = pl.BlockSpec(memory_space=pltpu.VMEM)
    hbm = pl.BlockSpec(memory_space=pltpu.MemorySpace.HBM)
    piece = (CHUNK * PER, taps)

    stacks, best = pl.pallas_call(
        functools.partial(kernel, n_tm, n_lib),
        out_shape=(
            jax.ShapeDtypeStruct((rounds, block, samples), bf),
            jax.ShapeDtypeStruct((per_dev, LANES), f32),
        ),
        in_specs=[hbm] * 5,
        out_specs=(vmem, vmem),
        scratch_shapes=[
            vm((channels, samples), bf),
            pltpu.SMEM(owner.shape, jnp.int32),
            pltpu.SMEM(slot.shape, jnp.int32),
            pltpu.SMEM(mask.shape, jnp.int32),
            vm(templates.shape[2:], bf),
            vm((chunks, SIDE, SIDE, *piece), bf),
            vm((chunks, SIDE - 1, SIDE, *piece), bf),
            vm((chunks, SIDE, *piece), bf),
            vm((chunks, SIDE - 1, *piece), bf),
            vm((n_tm, 2, per_dev // 2, channels, LANES), bf),
            vm(((rows + 2) * channels, LANES), f32),
            vm((2, rows + 2, channels, LANES), bf),
            vm((channels, 3 * LANES, 2 * LANES), bf),
            vm((channels, SHIFTS * PER, 3 * LANES), bf),
            vm((rows * channels, LANES), f32),
            vm((channels, 2, SHIFTS, LANES), f32),
            vm((rows * PER, LANES), f32),
            vm((2, SHIFTS * PER, LANES), f32),
            vm((n_tm, PER, samples), bf),
            vm((SIDE, SIDE * per_dev, LANES), f32),
            vm((SIDE * SIDE - 1, SIDE * per_dev, LANES), f32),
            vm((SIDE, per_dev, LANES), f32),
            vm((SIDE * near - 1, per_dev, LANES), f32),
            dma((5,)),
            dma((3,)), dma((3,)), dma((3,)), dma((3,)),
            dma((chunks, 3)), dma((chunks, 3)), dma((chunks, 3)), dma((chunks, 3)),
            dma((n_tm - 1,)), dma((n_tm - 1,)), dma((SIDE * SIDE - 1,)), dma((SIDE * SIDE - 1,)),
            dma((SIDE * near - 1,)), dma((SIDE * near - 1,)), dma, dma, pltpu.SemaphoreType.REGULAR,
        ],
        compiler_params=pltpu.CompilerParams(
            collective_id=0, has_side_effects=True, vmem_limit_bytes=48 << 20
        ),
        name="match",
    )(*(pltpu.with_memory_space_constraint(a, pltpu.MemorySpace.HBM) for a in (record, templates[0, 0], owner, slot, mask)))
    return stacks[None], best.reshape(samples)


def solution(mesh):
    placed = (
        P(None, "tm"),
        P("lib", "tm", None, None, None, None),
        P("lib", None),
        P("lib", None),
        P(),
    )
    return jax.shard_map(
        on_device,
        mesh=mesh,
        in_specs=placed,
        out_specs=(P("lib", None, None, "tm"), P("tm")),
        check_vma=False,
    )
```
